32 devices in a mesh: space: 4 (over y, core), vel: 8 (over z, x).
Axes of the slice: x: 2, y: 2, z: 4, core: 2. Of those that a mesh axis runs over, the one named last changes fastest.
Arguments:
- distribution: float32 [64, 48, 2304], P('space', 'vel'), may hold values from 0 to 2
- collision_rate: float32 [64], P('space'), may hold values from 0.1 to 1
- face_flags: int32 [64], replicated, may hold values 0 or 1
Outputs:
- updated: float32 [64, 48, 2304], P('space', 'vel')
The draws below stay inside these ranges and needn't reach their ends.
All inputs are finite; a program needn't handle non-finite values.
Results may differ from the reference program's by a relative error of at most 0.0001.
Values sent between devices are 32-bit elements; how exact they have to be, the bound alone decides.
A program may use at most 64 MiB of HBM per device.

```python
import math
import jax
import jax.numpy as jnp
from jax import lax

NV = 48
NCELLS = 64


def place_ends(array, own_key, smallest, high):
    longest = array.shape.index(max(array.shape))
    spots = []
    for shift in (0, 1):
        where = [jax.random.randint(jax.random.fold_in(own_key, axis), (), 0, length) for axis, length in enumerate(array.shape)]
        where[longest] = (where[longest] + shift) % array.shape[longest]
        spots.append(tuple(where))
    return array.at[spots[0]].set(smallest).at[spots[1]].set(high)


def steps_of(rng, extent, cuts, low, top_value):
    level, own = 1.0, jax.random.fold_in(rng, 6)
    for axis_at, parts in cuts:
        heights = jnp.exp(jax.random.uniform(jax.random.fold_in(own, axis_at), (parts,), jnp.float32, low / len(cuts), top_value / len(cuts)))
        level = level * jnp.repeat(heights, extent[axis_at] // parts).reshape([-1 if axis == axis_at else 1 for axis in range(len(extent))])
    return level


def setup_inputs(seed: int = 0) -> dict:
    key_list = jax.random.split(jax.random.key(seed), 4)
    distribution = jnp.clip(2.0 * jax.random.uniform(key_list[0], (NCELLS, NV, NV * NV), jnp.float32) ** steps_of(key_list[0], (NCELLS, NV, NV * NV), ((0, 4), (1, 8)), -0.2, 0.2), 0.0, 2.0)
    collision_rate = jnp.clip(jnp.exp(math.log(1.0) - 2.3025851 * jax.random.uniform(key_list[1], (NCELLS,), jnp.float32) ** steps_of(key_list[1], (NCELLS,), ((0, 4),), -0.2, 0.2)), 0.1, 1.0)
    face_flags = place_ends((jax.random.randint(key_list[2], (NCELLS,), 0, 16) < 1).astype(jnp.int32), jax.random.fold_in(key_list[2], 1), 0, 1)
    return dict(distribution=distribution, collision_rate=collision_rate, face_flags=face_flags)


LENGTH = 8.0
RADIUS = 6.0
COURANT = 0.9
GOLDEN = (1.0 + math.sqrt(5.0)) / 2.0
DIRECTIONS = ((0.0, 1.0, GOLDEN), (0.0, -1.0, GOLDEN), (1.0, GOLDEN, 0.0), (-1.0, GOLDEN, 0.0), (GOLDEN, 0.0, 1.0), (-GOLDEN, 0.0, 1.0))

def kernel_tables(points):
    index = jnp.arange(points, dtype=jnp.int32)
    wrapped = jnp.where(index < points // 2, index, jnp.where(index == points // 2, 0, index - points))
    signed = wrapped.astype(jnp.float32) * (math.pi / LENGTH)
    wave_z = signed[:, None, None]
    wave_x = signed[None, :, None]
    wave_y = signed[None, None, :]
    square = wave_x * wave_x + wave_y * wave_y + wave_z * wave_z
    scale = math.sqrt(1.0 + GOLDEN * GOLDEN)
    gain_tables = []
    loss_tables = []
    for direction in DIRECTIONS:
        parallel = (wave_x * direction[0] + wave_y * direction[1] + wave_z * direction[2]) / scale
        across = jnp.sqrt(jnp.maximum(square - parallel * parallel, 0.0))
        gain_tables.append(jnp.cos(0.5 * RADIUS * parallel))
        loss_tables.append(jnp.sinc(RADIUS * across / (2.0 * math.pi)))
    loss_total = sum(loss_tables) / 6.0
    return (gain_tables, loss_tables, loss_total)

def reference(distribution, collision_rate, face_flags):
    points = NV
    width = points * points
    cell_count = distribution.shape[0]
    gain_tables, loss_tables, loss_total = kernel_tables(points)

    def cell_term(one_cell):
        cube = one_cell.reshape(points, points, points)
        spectrum = jnp.fft.fftn(cube)
        products = []
        for gain_table, loss_table in zip(gain_tables, loss_tables):
            first_part = jnp.fft.ifftn(spectrum * gain_table).real
            second_part = jnp.fft.ifftn(spectrum * loss_table).real
            products.append(first_part * second_part)
        gain_total = sum(products) / 6.0
        loss_part = cube * jnp.fft.ifftn(spectrum * loss_total).real
        return (gain_total - loss_part).reshape(points, width)
    collision = lax.map(cell_term, distribution)
    mirror = distribution.reshape(cell_count, points, points, points)[:, :, ::-1, :].reshape(cell_count, points, width)
    previous = jnp.concatenate([distribution[:1], distribution[:-1]], axis=0)
    following = jnp.concatenate([distribution[1:], distribution[-1:]], axis=0)
    wall_flags = jnp.concatenate([face_flags, jnp.ones((1,), jnp.int32)])
    lower_wall = (wall_flags[:-1] == 1)[:, None, None]
    upper_wall = (wall_flags[1:] == 1)[:, None, None]
    lower_side = jnp.where(lower_wall, mirror, previous)
    upper_side = jnp.where(upper_wall, mirror, following)
    column = (jnp.arange(width, dtype=jnp.int32) // points).astype(jnp.float32)
    centre = (points - 1) / 2.0
    speed = COURANT * (column - centre) / centre
    upwind_flux = jnp.where(speed > 0, speed * (distribution - lower_side), speed * (upper_side - distribution))
    return distribution - upwind_flux + collision_rate[:, None, None] * collision
```

```python
import functools
import math

import jax
import jax.numpy as jnp
import ml_dtypes
import numpy as np
from jax import lax
from jax.experimental import pallas as pl
from jax.experimental.pallas import tpu as pltpu
from jax.sharding import PartitionSpec as P

NV = 48
LENGTH = 8.0
RADIUS = 6.0
COURANT = 0.9
GOLDEN = (1.0 + math.sqrt(5.0)) / 2.0
SCALE = math.sqrt(1.0 + GOLDEN * GOLDEN)
HALF = 64
LANES = 128
FOLD = NV // 2
PLANES = 12
CHUNKS = NV // PLANES
ROWS = PLANES * FOLD
BLOCKS = ROWS // NV
GROUP = 4
BF = jnp.bfloat16
MESH = pl.DeviceIdType.MESH


def real_basis():
    j = np.arange(NV)
    q = np.zeros((NV, NV))
    for f in range(25):
        q[f] = np.cos(2 * np.pi * f * j / NV) * (1.0 if f in (0, 24) else math.sqrt(2.0))
    for f in range(1, 24):
        q[24 + f] = np.sin(2 * np.pi * f * j / NV) * math.sqrt(2.0)
    q /= math.sqrt(NV)
    odd = np.zeros((NV, NV))
    for f in range(1, 24):
        odd[:, f] = -q[24 + f]
        odd[:, 24 + f] = q[f]
    mag = np.concatenate([np.arange(24), [0], np.arange(1, 24)]) * (math.pi / LENGTH)
    return q, odd, mag


def circulants():
    j = np.arange(NV)
    k = np.where(j < 24, j, np.where(j == 24, 0, j - NV))
    xi = k * (math.pi / LENGTH)
    f = np.fft.fft(np.eye(NV), axis=0)

    def real(mult):
        return np.real(np.fft.ifft(mult[:, None] * f, axis=0))

    result = []
    for length in (1.0 / SCALE, GOLDEN / SCALE):
        angle = 0.5 * RADIUS * xi * length
        result.append((real(np.cos(angle)), real(1j * np.sin(angle))))
    return result


def split_np(w):
    w = np.asarray(w, np.float32)
    hi = w.astype(ml_dtypes.bfloat16)
    lo = (w - hi.astype(np.float32)).astype(ml_dtypes.bfloat16)
    return hi, lo


def left(w):
    hi, lo = split_np(w)
    return np.concatenate([hi, hi, lo], axis=1)


def right(blocks):
    full = np.zeros((LANES, LANES))
    for i in range(2):
        for j in range(2):
            full[i * HALF : i * HALF + NV, j * HALF : j * HALF + NV] = blocks[i][j].T
    hi, lo = split_np(full)
    return np.concatenate([hi, hi, lo], axis=0)


def apart(w):
    return right([[w, 0 * w], [0 * w, w]])


def crossed(w):
    return right([[w, w], [w, -w]])


def pair_left(even, odd):
    none = np.zeros((FOLD, FOLD))
    return np.block([[even, none], [none, even], [odd, none], [none, odd]])


def build_tables():
    q, odd, mag = real_basis()
    (c1, d1), (c2, d2) = circulants()
    freq = np.concatenate([np.arange(25), np.arange(1, 24)])
    ie, io = np.where(freq % 2 == 0)[0], np.where(freq % 2 == 1)[0]
    mz, mx, my = mag[:, None, None], mag[None, :, None], mag[None, None, :]
    square = mz * mz + mx * mx + my * my

    def sinc(p):
        return np.sinc(RADIUS * np.sqrt(np.maximum(square - p * p, 0.0)) / (2.0 * math.pi))

    plus, minus = [], []
    for first, second in ((my, mz), (mx, my), (mz, mx)):
        same = sinc((first + GOLDEN * second) / SCALE)
        other = sinc((GOLDEN * second - first) / SCALE)
        plus.append((same + other) / 6.0)
        minus.append((other - same) / 6.0)
    values = np.stack(plus + minus).transpose(0, 2, 1, 3)
    spec = np.zeros((6, FOLD, NV, LANES), np.float32)
    spec[..., :NV] = values[:, ie]
    spec[..., HALF : HALF + NV] = values[:, io]

    def ring(c):
        a, b = c[:FOLD, :FOLD], c[:FOLD, FOLD:]
        return pair_left((a + b) / 2.0, (a - b) / 2.0)

    along_z = np.stack([left(w) for w in (q, q.T, odd, c2, d2, c1, d1)])
    along_x = np.stack(
        [
            left(pair_left(q[ie, :FOLD], q[io, :FOLD])),
            left(pair_left(q.T[:FOLD, ie], q.T[:FOLD, io])),
            left(pair_left(odd[:FOLD, ie], odd[:FOLD, io])),
        ]
    )
    gain_x = left(np.concatenate([ring(c1), ring(d1), ring(c2), ring(d2)], axis=0))
    right_first = np.concatenate([crossed(q), apart(c1), apart(d1)], axis=1)
    right_rest = np.stack([crossed(w) for w in (c2, d2, q.T, odd)])
    speed = np.abs(COURANT * (np.arange(NV) - (NV - 1) / 2.0) / ((NV - 1) / 2.0))
    fold = np.zeros((FOLD, LANES), np.float32)
    fold[:, :HALF] = speed[:FOLD, None]
    fold[:, HALF:] = speed[FOLD:, None]
    flat = np.broadcast_to(np.repeat(speed, NV), (8, NV * NV)).astype(np.float32)
    return spec, along_z, along_x, gain_x, right_first, right_rest, np.tile(fold, (2, 1)), flat


def parts(x):
    hi = x.astype(BF)
    lo = (x - hi.astype(jnp.float32)).astype(BF)
    return hi, lo


def tall(x):
    hi, lo = parts(x)
    return jnp.concatenate([hi, lo, hi], axis=0)


def wide(x):
    hi, lo = parts(x)
    return jnp.concatenate([hi, lo, hi], axis=1)


def dot(a, b):
    return jnp.dot(a, b, preferred_element_type=jnp.float32)


def lanes_of(rows):
    return lax.broadcasted_iota(jnp.int32, (rows, LANES), 1)


def turn(x, shift):
    shift %= LANES
    return pltpu.roll(x, shift, axis=1) if shift else x


def along(w, x):
    count = x.shape[0] // NV
    result = dot(w, jnp.concatenate([tall(x[i * NV : (i + 1) * NV]) for i in range(count)], axis=1))
    low = lanes_of(NV) < HALF
    fields = []
    for n in range(w.shape[0] // (2 * NV)):
        blocks = []
        for i in range(count):
            both = result[2 * NV * n : 2 * NV * (n + 1), i * LANES : (i + 1) * LANES]
            blocks.append(jnp.where(low, both[:NV], both[NV:]))
        fields.append(jnp.concatenate(blocks, axis=0))
    return fields


def cross(x):
    other = pltpu.roll(x, HALF, axis=1)
    return jnp.where(lanes_of(x.shape[0]) < HALF, other + x, other - x)


def unpack(block, u, um, start, planes):
    lane = lanes_of(planes)
    for xl in range(FOLD):
        tile, offset = divmod(NV * xl, LANES)
        pieces = []
        for side in range(2):
            t = tile + side * (NV * FOLD // LANES)
            piece = block[:, t * LANES : (t + 1) * LANES]
            if offset + NV > LANES:
                piece = jnp.where(lane >= offset, piece, block[:, (t + 1) * LANES : (t + 2) * LANES])
            pieces.append(turn(piece, side * HALF - offset))
        row = jnp.where(lane < HALF, pieces[0], pieces[1])
        u[pl.ds(start + xl, planes, stride=FOLD), :] = row
        um[pl.ds(start + FOLD - 1 - xl, planes, stride=FOLD), :] = turn(row, HALF)


def pack(read, write, planes):
    lane = lanes_of(planes)
    rows = [read(xl) for xl in range(FOLD)]
    for t in range(NV * FOLD // LANES):
        for side in range(2):
            tile = None
            for xl in range(t * LANES // NV, (t * LANES + LANES - 1) // NV + 1):
                offset = NV * xl - t * LANES
                piece = turn(rows[xl], offset - side * HALF)
                tile = piece if tile is None else jnp.where(lane >= offset, piece, tile)
            write(t + side * (NV * FOLD // LANES), tile)


def step_kernel(
    nspace, nvel, total, x_hbm, rate, flags, spec_hbm, lz, lx, gx, rf, rr, fold, flat, out,
    xv, stage, sback, back, halo, u, um, v, gains, pair, fields, term, spec,
    load_sem, in_send, in_recv, out_send, out_recv, own_in, own_out, halo_send, halo_recv,
):
    planes, cells, width = xv.shape
    own = cells // nvel
    half = width // 2
    per = PLANES // planes
    sp, me = lax.axis_index("space"), lax.axis_index("vel")
    after, before = lax.rem(sp + 1, nspace), lax.rem(sp + nspace - 1, nspace)
    barrier = pltpu.get_barrier_semaphore()

    load_x = pltpu.make_async_copy(x_hbm, xv, load_sem.at[0])
    load_x.start()
    load_spec = pltpu.make_async_copy(spec_hbm, spec, load_sem.at[1])
    load_spec.start()
    for r in range(1, nvel):
        peer = jnp.bitwise_xor(me, r)
        pl.semaphore_signal(barrier, inc=1, device_id=(sp, peer), device_id_type=MESH)
    pl.semaphore_signal(barrier, inc=1, device_id=(after, me), device_id_type=MESH)
    pl.semaphore_signal(barrier, inc=1, device_id=(before, me), device_id_type=MESH)
    load_x.wait()
    pl.semaphore_wait(barrier, nvel + 1)

    def sending(c, m, r, peer, row):
        return pltpu.make_async_remote_copy(
            src_ref=xv.at[:, row, :], dst_ref=stage.at[c, m],
            send_sem=in_send.at[c, r], recv_sem=in_recv.at[c, r],
            device_id=(sp, peer), device_id_type=MESH,
        )

    def start_in(c):
        for m in range(nvel):
            @pl.when(me == m)
            def _():
                for r in range(1, nvel):
                    sending(c, m, r, m ^ r, c * nvel + (m ^ r)).start()
                pltpu.make_async_copy(
                    xv.at[:, c * nvel + m, :], stage.at[c, m], own_in.at[c]
                ).start()

    start_in(0)
    halos = [
        pltpu.make_async_remote_copy(
            src_ref=xv.at[:, cells - 1, pl.ds(half, half)], dst_ref=halo.at[0],
            send_sem=halo_send.at[0], recv_sem=halo_recv.at[0],
            device_id=(after, me), device_id_type=MESH,
        ),
        pltpu.make_async_remote_copy(
            src_ref=xv.at[:, 0, pl.ds(0, half)], dst_ref=halo.at[1],
            send_sem=halo_send.at[1], recv_sem=halo_recv.at[1],
            device_id=(before, me), device_id_type=MESH,
        ),
    ]
    for copy in halos:
        copy.start()

    def lower_wall(cell):
        return flags[cell] == 1

    def upper_wall(cell):
        return jnp.logical_or(cell + 1 >= total, flags[jnp.minimum(cell + 1, total - 1)] == 1)

    row_of = lax.broadcasted_iota(jnp.int32, (cells, LANES), 0)
    keep_lower = jnp.zeros((cells, LANES), jnp.float32)
    keep_upper = jnp.zeros((cells, LANES), jnp.float32)
    for c in range(cells):
        cell = sp * cells + c
        low = jnp.where(lower_wall(cell), 0.0, 1.0)
        high = jnp.where(upper_wall(cell), 0.0, 1.0)
        keep_lower = jnp.where(row_of == c, low, keep_lower)
        keep_upper = jnp.where(row_of == c, high, keep_upper)
    at_first = jnp.where(sp == 0, 1.0, 0.0)
    for copy in halos:
        copy.wait()

    for z in range(planes):
        for t in range(width // LANES):
            cut = slice(t * LANES, (t + 1) * LANES)
            value = xv[z, :, cut]
            weight = jnp.concatenate([flat[:, cut]] * (cells // 8), axis=0)
            if t >= half // LANES:
                edge = halo[0, z : z + 1, t * LANES - half : (t + 1) * LANES - half]
                edge = edge + at_first * (value[:1] - edge)
                near = jnp.where(row_of == 0, edge, pltpu.roll(value, 1, axis=0))
                keep = keep_lower
            else:
                edge = halo[1, z : z + 1, cut]
                near = jnp.where(row_of == cells - 1, edge, pltpu.roll(value, cells - 1, axis=0))
                keep = keep_upper
            out[z, :, cut] = value - weight * (value - keep * near)

    for c in range(1, own):
        for r in range(1, nvel):
            sending(c - 1, me, r, jnp.bitwise_xor(me, r), 0).wait_send()
        start_in(c)
    load_spec.wait()

    low_lanes = lanes_of(1) < HALF
    mine = me // per

    def cell_step(c, carry):
        cell = sp * cells + c * nvel + me
        speed_rate = rate[c * nvel + me]
        wall = jnp.where(
            low_lanes,
            jnp.where(upper_wall(cell), 1.0, 0.0),
            jnp.where(lower_wall(cell), 1.0, 0.0),
        )

        def first(k, carry):
            chunk = jnp.bitwise_xor(mine, k)
            for p in range(per):
                slab = chunk * per + p

                @pl.when(slab != me)
                def _():
                    r = jnp.bitwise_xor(slab, me)
                    sending(c, slab, r, slab, 0).wait_recv()

                @pl.when(slab == me)
                def _():
                    pltpu.make_async_copy(xv.at[:, 0, :], stage.at[c, me], own_in.at[c]).wait()

                unpack(stage.at[c, slab], u, um, slab * (planes * FOLD), planes)
            rows = pl.ds(pl.multiple_of(chunk * ROWS, ROWS), ROWS)
            value = u[rows, :]
            three = dot(wide(value), rf[...])
            gains[0, rows, :] = three[:, LANES : 2 * LANES]
            gains[1, rows, :] = three[:, 2 * LANES :]
            v[rows, :] = along(lx[0], three[:, :LANES])[0]
            g1, g2, g3, g4 = along(gx[...], cross(value))
            pair[0, rows, :] = dot(wide(g1), rr[0])
            pair[1, rows, :] = dot(wide(g2), rr[1])
            gains[2, rows, :] = g3
            gains[3, rows, :] = g4
            return carry

        lax.fori_loop(0, CHUNKS, first, 0)

        def second(k, carry):
            cuts = [pl.ds(k * GROUP + i, NV, stride=FOLD) for i in range(GROUP)]
            s = dot(lz[0], jnp.concatenate([tall(v[cut, :]) for cut in cuts], axis=1))
            for order, w in (((0, 1, 2, 4), 1), ((3, 5), 2)):
                hats = [
                    tall(s[:, i * LANES : (i + 1) * LANES] * spec[f, k * GROUP + i])
                    for f in order
                    for i in range(GROUP)
                ]
                result = dot(lz[w], jnp.concatenate(hats, axis=1))
                for n, f in enumerate(order):
                    for i in range(GROUP):
                        at = (n * GROUP + i) * LANES
                        fields[f, cuts[i], :] = result[:, at : at + LANES]
            for n in range(4):
                value = jnp.concatenate([tall(gains[n, cut, :]) for cut in cuts], axis=1)
                result = dot(lz[3 + n], value)
                for i in range(GROUP):
                    gains[n, cuts[i], :] = result[:, i * LANES : (i + 1) * LANES]
            return carry

        lax.fori_loop(0, FOLD // GROUP, second, 0)

        def third(k, carry):
            chunk = jnp.bitwise_xor(mine, CHUNKS - 1 - k)
            rows = pl.ds(pl.multiple_of(chunk * ROWS, ROWS), ROWS)
            even_x = along(lx[1], jnp.concatenate([fields[f, rows, :] for f in (0, 1, 2, 3)], axis=0))[0]
            odd_x = along(lx[2], jnp.concatenate([fields[f, rows, :] for f in (4, 5)], axis=0))[0]
            even = dot(wide(jnp.concatenate([even_x[: 3 * ROWS], odd_x[ROWS:]], axis=0)), rr[2])
            odd = dot(wide(jnp.concatenate([even_x[3 * ROWS :], odd_x[:ROWS]], axis=0)), rr[3])
            value = u[rows, :]
            result = (gains[0, rows, :] - value) * even[:ROWS]
            result += gains[1, rows, :] * odd[:ROWS]
            result += (pair[0, rows, :] - value) * even[ROWS : 2 * ROWS]
            result += pair[1, rows, :] * odd[ROWS:]
            result += (cross(gains[2, rows, :]) - value) * even[2 * ROWS : 3 * ROWS]
            result += cross(gains[3, rows, :]) * even[3 * ROWS :]
            weight = jnp.concatenate([fold[...]] * BLOCKS, axis=0)
            term[...] = speed_rate * result + wall * weight * um[rows, :]
            for p in range(per):
                slab = chunk * per + p

                def write(t, tile):
                    sback[c, slab, :, t * LANES : (t + 1) * LANES] = tile

                pack(
                    lambda xl: term[pl.ds(p * planes * FOLD + xl, planes, stride=FOLD), :],
                    write, planes,
                )
                for m in range(nvel):
                    @pl.when(jnp.logical_and(me == m, slab != m))
                    def _():
                        pltpu.make_async_remote_copy(
                            src_ref=sback.at[c, slab], dst_ref=back.at[c, :, m, :],
                            send_sem=out_send.at[c, jnp.bitwise_xor(slab, m)],
                            recv_sem=out_recv.at[c, jnp.bitwise_xor(slab, m)],
                            device_id=(sp, slab), device_id_type=MESH,
                        ).start()

                    @pl.when(jnp.logical_and(me == m, slab == m))
                    def _():
                        pltpu.make_async_copy(
                            sback.at[c, m], back.at[c, :, m, :], own_out.at[c]
                        ).start()
            return carry

        lax.fori_loop(0, CHUNKS, third, 0)
        return carry

    lax.fori_loop(0, own, cell_step, 0)
    for r in range(1, nvel):
        sending(own - 1, me, r, jnp.bitwise_xor(me, r), 0).wait_send()
    for c in range(own):
        for r in range(1, nvel):
            peer = jnp.bitwise_xor(me, r)
            copy = pltpu.make_async_remote_copy(
                src_ref=sback.at[c, peer], dst_ref=back.at[c, :, 0, :],
                send_sem=out_send.at[c, r], recv_sem=out_recv.at[c, r],
                device_id=(sp, peer), device_id_type=MESH,
            )
            copy.wait_send()
            copy.wait_recv()
        pltpu.make_async_copy(sback.at[c, me], back.at[c, :, 0, :], own_out.at[c]).wait()
        cut = slice(c * nvel, (c + 1) * nvel)
        for z in range(planes):
            out[z, cut, :] = out[z, cut, :] + back[c, z]


def solution(mesh):
    nspace, nvel = mesh.shape["space"], mesh.shape["vel"]
    tables = build_tables()

    def body(distribution, collision_rate, face_flags):
        cells, planes, width = distribution.shape
        own = cells // nvel
        vmem, smem = (pl.BlockSpec(memory_space=s) for s in (pltpu.VMEM, pltpu.SMEM))
        anywhere = pl.BlockSpec(memory_space=pl.ANY)
        size = (NV * FOLD, LANES)
        f32 = jnp.float32
        dma = pltpu.SemaphoreType.DMA
        result = pl.pallas_call(
            functools.partial(step_kernel, nspace, nvel, nspace * cells),
            out_shape=jax.ShapeDtypeStruct((planes, cells, width), f32),
            in_specs=[anywhere, smem, smem, anywhere] + [vmem] * 7,
            out_specs=vmem,
            scratch_shapes=[
                pltpu.VMEM((planes, cells, width), f32),
                pltpu.VMEM((own, nvel, planes, width), f32),
                pltpu.VMEM((own, nvel, planes, width), f32),
                pltpu.VMEM((own, planes, nvel, width), f32),
                pltpu.VMEM((2, planes, width // 2), f32),
                pltpu.VMEM(size, f32),
                pltpu.VMEM(size, f32),
                pltpu.VMEM(size, f32),
                pltpu.VMEM((4,) + size, f32),
                pltpu.VMEM((2,) + size, f32),
                pltpu.VMEM((6,) + size, f32),
                pltpu.VMEM((ROWS, LANES), f32),
                pltpu.VMEM((6, FOLD, NV, LANES), f32),
                dma((2,)),
                dma((own, nvel)),
                dma((own, nvel)),
                dma((own, nvel)),
                dma((own, nvel)),
                dma((own,)),
                dma((own,)),
                dma((2,)),
                dma((2,)),
            ],
            compiler_params=pltpu.CompilerParams(
                collective_id=0, has_side_effects=True, vmem_limit_bytes=48 * 1024 * 1024
            ),
            cost_estimate=pl.CostEstimate(
                flops=10**9, bytes_accessed=10 * 2**20, transcendentals=0
            ),
        )(
            jnp.transpose(distribution, (1, 0, 2)), collision_rate, face_flags,
            *[jnp.asarray(t) for t in tables],
        )
        return jnp.transpose(result, (1, 0, 2))

    return jax.shard_map(
        body,
        mesh=mesh,
        in_specs=(P("space", "vel", None), P("space"), P()),
        out_specs=P("space", "vel", None),
        check_vma=False,
    )
```

```python
import functools
import math

import jax
import jax.numpy as jnp
import ml_dtypes
import numpy as np
from jax import lax
from jax.experimental import pallas as pl
from jax.experimental.pallas import tpu as pltpu
from jax.sharding import PartitionSpec as P

NV = 48
LENGTH = 8.0
RADIUS = 6.0
COURANT = 0.9
GOLDEN = (1.0 + math.sqrt(5.0)) / 2.0
SCALE = math.sqrt(1.0 + GOLDEN * GOLDEN)
HALF = 64
LANES = 128
FOLD = NV // 2
PLANES = 12
CHUNKS = NV // PLANES
ROWS = PLANES * FOLD
BLOCKS = ROWS // NV
GROUP = 4
BF = jnp.bfloat16
MESH = pl.DeviceIdType.MESH


def real_basis():
    j = np.arange(NV)
    q = np.zeros((NV, NV))
    for f in range(25):
        q[f] = np.cos(2 * np.pi * f * j / NV) * (1.0 if f in (0, 24) else math.sqrt(2.0))
    for f in range(1, 24):
        q[24 + f] = np.sin(2 * np.pi * f * j / NV) * math.sqrt(2.0)
    q /= math.sqrt(NV)
    odd = np.zeros((NV, NV))
    for f in range(1, 24):
        odd[:, f] = -q[24 + f]
        odd[:, 24 + f] = q[f]
    mag = np.concatenate([np.arange(24), [0], np.arange(1, 24)]) * (math.pi / LENGTH)
    return q, odd, mag


def circulants():
    j = np.arange(NV)
    k = np.where(j < 24, j, np.where(j == 24, 0, j - NV))
    xi = k * (math.pi / LENGTH)
    f = np.fft.fft(np.eye(NV), axis=0)

    def real(mult):
        return np.real(np.fft.ifft(mult[:, None] * f, axis=0))

    result = []
    for length in (1.0 / SCALE, GOLDEN / SCALE):
        angle = 0.5 * RADIUS * xi * length
        result.append((real(np.cos(angle)), real(1j * np.sin(angle))))
    return result


def split_np(w):
    w = np.asarray(w, np.float32)
    hi = w.astype(ml_dtypes.bfloat16)
    lo = (w - hi.astype(np.float32)).astype(ml_dtypes.bfloat16)
    return hi, lo


def left(w):
    hi, lo = split_np(w)
    return np.concatenate([hi, hi, lo], axis=1)


def right(blocks):
    full = np.zeros((LANES, LANES))
    for i in range(2):
        for j in range(2):
            full[i * HALF : i * HALF + NV, j * HALF : j * HALF + NV] = blocks[i][j].T
    hi, lo = split_np(full)
    return np.concatenate([hi, hi, lo], axis=0)


def apart(w):
    return right([[w, 0 * w], [0 * w, w]])


def crossed(w):
    return right([[w, w], [w, -w]])


def pair_left(even, odd):
    none = np.zeros((FOLD, FOLD))
    return np.block([[even, none], [none, even], [odd, none], [none, odd]])


def build_tables():
    q, odd, mag = real_basis()
    (c1, d1), (c2, d2) = circulants()
    freq = np.concatenate([np.arange(25), np.arange(1, 24)])
    ie, io = np.where(freq % 2 == 0)[0], np.where(freq % 2 == 1)[0]
    mz, mx, my = mag[:, None, None], mag[None, :, None], mag[None, None, :]
    square = mz * mz + mx * mx + my * my

    def sinc(p):
        return np.sinc(RADIUS * np.sqrt(np.maximum(square - p * p, 0.0)) / (2.0 * math.pi))

    plus, minus = [], []
    for first, second in ((my, mz), (mx, my), (mz, mx)):
        same = sinc((first + GOLDEN * second) / SCALE)
        other = sinc((GOLDEN * second - first) / SCALE)
        plus.append((same + other) / 6.0)
        minus.append((other - same) / 6.0)
    values = np.stack(plus + minus).transpose(0, 2, 1, 3)
    spec = np.zeros((6, FOLD, NV, LANES), np.float32)
    spec[..., :NV] = values[:, ie]
    spec[..., HALF : HALF + NV] = values[:, io]

    def ring(c):
        a, b = c[:FOLD, :FOLD], c[:FOLD, FOLD:]
        return pair_left((a + b) / 2.0, (a - b) / 2.0)

    along_z = np.stack([left(w) for w in (q, q.T, odd, c2, d2, c1, d1)])
    along_x = np.stack(
        [
            left(pair_left(q[ie, :FOLD], q[io, :FOLD])),
            left(pair_left(q.T[:FOLD, ie], q.T[:FOLD, io])),
            left(pair_left(odd[:FOLD, ie], odd[:FOLD, io])),
        ]
    )
    gain_x = left(np.concatenate([ring(c1), ring(d1), ring(c2), ring(d2)], axis=0))
    right_first = np.concatenate([crossed(q), apart(c1), apart(d1)], axis=1)
    right_rest = np.stack([crossed(w) for w in (c2, d2, q.T, odd)])
    speed = np.abs(COURANT * (np.arange(NV) - (NV - 1) / 2.0) / ((NV - 1) / 2.0))
    fold = np.zeros((FOLD, LANES), np.float32)
    fold[:, :HALF] = speed[:FOLD, None]
    fold[:, HALF:] = speed[FOLD:, None]
    flat = np.broadcast_to(np.repeat(speed, NV), (8, NV * NV)).astype(np.float32)
    single = np.concatenate(
        [
            spec.reshape(-1, LANES),
            np.tile(fold, (2, 1)),
            flat.reshape(8, -1, LANES).transpose(1, 0, 2).reshape(-1, LANES),
        ]
    )

    def padded(w):
        w = w.reshape(-1, w.shape[-1])
        return np.pad(w, ((0, 3 * LANES - w.shape[0]), (0, 2 * LANES - w.shape[1])))

    halves = np.concatenate(
        [right_first, *right_rest, padded(gain_x), padded(along_x), padded(along_z)], axis=1
    )
    return single, halves


SPEC_ROWS = 6 * FOLD * NV
DEPTH = 3 * NV


def parts(x):
    hi = x.astype(BF)
    lo = (x - hi.astype(jnp.float32)).astype(BF)
    return hi, lo


def tall(x):
    hi, lo = parts(x)
    return jnp.concatenate([hi, lo, hi], axis=0)


def wide(x):
    hi, lo = parts(x)
    return jnp.concatenate([hi, lo, hi], axis=1)


def dot(a, b):
    return jnp.dot(a, b, preferred_element_type=jnp.float32)


def lanes_of(rows):
    return lax.broadcasted_iota(jnp.int32, (rows, LANES), 1)


def turn(x, shift):
    shift %= LANES
    return pltpu.roll(x, shift, axis=1) if shift else x


def along(w, x):
    count = x.shape[0] // NV
    result = dot(w, jnp.concatenate([tall(x[i * NV : (i + 1) * NV]) for i in range(count)], axis=1))
    low = lanes_of(NV) < HALF
    fields = []
    for n in range(w.shape[0] // (2 * NV)):
        blocks = []
        for i in range(count):
            both = result[2 * NV * n : 2 * NV * (n + 1), i * LANES : (i + 1) * LANES]
            blocks.append(jnp.where(low, both[:NV], both[NV:]))
        fields.append(jnp.concatenate(blocks, axis=0))
    return fields


def cross(x):
    other = pltpu.roll(x, HALF, axis=1)
    return jnp.where(lanes_of(x.shape[0]) < HALF, other + x, other - x)


def unpack(block, u, um, start, planes):
    lane = lanes_of(planes)
    for xl in range(FOLD):
        tile, offset = divmod(NV * xl, LANES)
        pieces = []
        for side in range(2):
            t = tile + side * (NV * FOLD // LANES)
            piece = block[:, t * LANES : (t + 1) * LANES]
            if offset + NV > LANES:
                piece = jnp.where(lane >= offset, piece, block[:, (t + 1) * LANES : (t + 2) * LANES])
            pieces.append(turn(piece, side * HALF - offset))
        row = jnp.where(lane < HALF, pieces[0], pieces[1])
        u[pl.ds(start + xl, planes, stride=FOLD), :] = row
        um[pl.ds(start + FOLD - 1 - xl, planes, stride=FOLD), :] = turn(row, HALF)


def pack(read, write, planes):
    lane = lanes_of(planes)
    rows = [read(xl) for xl in range(FOLD)]
    for t in range(NV * FOLD // LANES):
        for side in range(2):
            tile = None
            for xl in range(t * LANES // NV, (t * LANES + LANES - 1) // NV + 1):
                offset = NV * xl - t * LANES
                piece = turn(rows[xl], offset - side * HALF)
                tile = piece if tile is None else jnp.where(lane >= offset, piece, tile)
            write(t + side * (NV * FOLD // LANES), tile)


def step_kernel(
    nspace, nvel, total, *refs,
):
    (
        x_hbm, rate_hbm, flags_hbm, single_hbm, halves_hbm, out,
        xv, stage, sback, back, halo, u, um, v, gains, pair, fields, term,
        rate, flags, single, halves,
        load_sem, in_send, in_recv, out_send, out_recv, own_in, own_out, halo_send, halo_recv,
    ) = refs
    planes, cells, width = xv.shape
    own = cells // nvel
    half = width // 2
    per = PLANES // planes
    sp, me = lax.axis_index("space"), lax.axis_index("vel")
    after, before = lax.rem(sp + 1, nspace), lax.rem(sp + nspace - 1, nspace)
    barrier = pltpu.get_barrier_semaphore()

    def load(i, source, target):
        return pltpu.make_async_copy(source, target, load_sem.at[i])

    first_x = [
        load(c, x_hbm.at[:, pl.ds(c * (cells // own), cells // own)], xv.at[:, pl.ds(c * (cells // own), cells // own)])
        for c in range(own)
    ]
    tables = [
        load(own, single_hbm, single),
        load(own + 1, halves_hbm, halves),
        load(own + 2, rate_hbm, rate),
        load(own + 3, flags_hbm, flags),
    ]
    first_x[0].start()
    for r in range(1, nvel):
        peer = jnp.bitwise_xor(me, r)
        pl.semaphore_signal(barrier, inc=1, device_id=(sp, peer), device_id_type=MESH)
    pl.semaphore_signal(barrier, inc=1, device_id=(after, me), device_id_type=MESH)
    pl.semaphore_signal(barrier, inc=1, device_id=(before, me), device_id_type=MESH)
    pl.semaphore_wait(barrier, nvel + 1)
    first_x[0].wait()

    def sending(c, m, r, peer, row):
        return pltpu.make_async_remote_copy(
            src_ref=xv.at[:, row, :], dst_ref=stage.at[c, m],
            send_sem=in_send.at[c, r], recv_sem=in_recv.at[c, r],
            device_id=(sp, peer), device_id_type=MESH,
        )

    def start_in(c):
        for m in range(nvel):
            @pl.when(me == m)
            def _():
                for r in range(1, nvel):
                    sending(c, m, r, m ^ r, c * nvel + (m ^ r)).start()
                pltpu.make_async_copy(
                    xv.at[:, c * nvel + m, :], stage.at[c, m], own_in.at[c]
                ).start()

    start_in(0)
    for copy in first_x[1:] + tables:
        copy.start()
    for copy in first_x[1:]:
        copy.wait()
    halos = [
        pltpu.make_async_remote_copy(
            src_ref=xv.at[:, cells - 1, pl.ds(half, half)], dst_ref=halo.at[0],
            send_sem=halo_send.at[0], recv_sem=halo_recv.at[0],
            device_id=(after, me), device_id_type=MESH,
        ),
        pltpu.make_async_remote_copy(
            src_ref=xv.at[:, 0, pl.ds(0, half)], dst_ref=halo.at[1],
            send_sem=halo_send.at[1], recv_sem=halo_recv.at[1],
            device_id=(before, me), device_id_type=MESH,
        ),
    ]
    for copy in halos:
        copy.start()
    for copy in tables:
        copy.wait()

    def lower_wall(cell):
        return flags[cell] == 1

    def upper_wall(cell):
        return jnp.logical_or(cell + 1 >= total, flags[jnp.minimum(cell + 1, total - 1)] == 1)

    row_of = lax.broadcasted_iota(jnp.int32, (cells, LANES), 0)
    keep_lower = jnp.zeros((cells, LANES), jnp.float32)
    keep_upper = jnp.zeros((cells, LANES), jnp.float32)
    for c in range(cells):
        cell = sp * cells + c
        low = jnp.where(lower_wall(cell), 0.0, 1.0)
        high = jnp.where(upper_wall(cell), 0.0, 1.0)
        keep_lower = jnp.where(row_of == c, low, keep_lower)
        keep_upper = jnp.where(row_of == c, high, keep_upper)
    at_first = jnp.where(sp == 0, 1.0, 0.0)
    for copy in halos:
        copy.wait()

    for z in range(planes):
        for t in range(width // LANES):
            cut = slice(t * LANES, (t + 1) * LANES)
            value = xv[z, :, cut]
            at = SPEC_ROWS + NV + 8 * t
            weight = jnp.concatenate([single[at : at + 8]] * (cells // 8), axis=0)
            if t >= half // LANES:
                edge = halo[0, z : z + 1, t * LANES - half : (t + 1) * LANES - half]
                edge = edge + at_first * (value[:1] - edge)
                near = jnp.where(row_of == 0, edge, pltpu.roll(value, 1, axis=0))
                keep = keep_lower
            else:
                edge = halo[1, z : z + 1, cut]
                near = jnp.where(row_of == cells - 1, edge, pltpu.roll(value, cells - 1, axis=0))
                keep = keep_upper
            out[z, :, cut] = value - weight * (value - keep * near)

    for c in range(1, own):
        for r in range(1, nvel):
            sending(c - 1, me, r, jnp.bitwise_xor(me, r), 0).wait_send()
        start_in(c)

    low_lanes = lanes_of(1) < HALF
    mine = me // per

    def lx(n):
        return halves[2 * NV * n : 2 * NV * (n + 1), 9 * LANES : 9 * LANES + DEPTH]

    def lz(n):
        return halves[NV * n : NV * (n + 1), 11 * LANES : 11 * LANES + DEPTH]

    def spectrum(f, xl):
        return single[pl.ds(pl.multiple_of((f * FOLD + xl) * NV, NV), NV), :]

    def cell_step(c, carry):
        cell = sp * cells + c * nvel + me
        speed_rate = rate[c * nvel + me]
        wall = jnp.where(
            low_lanes,
            jnp.where(upper_wall(cell), 1.0, 0.0),
            jnp.where(lower_wall(cell), 1.0, 0.0),
        )

        def first(k, carry):
            chunk = jnp.bitwise_xor(mine, k)
            for p in range(per):
                slab = chunk * per + p

                @pl.when(slab != me)
                def _():
                    r = jnp.bitwise_xor(slab, me)
                    sending(c, slab, r, slab, 0).wait_recv()

                @pl.when(slab == me)
                def _():
                    pltpu.make_async_copy(xv.at[:, 0, :], stage.at[c, me], own_in.at[c]).wait()

                unpack(stage.at[c, slab], u, um, slab * (planes * FOLD), planes)
            rows = pl.ds(pl.multiple_of(chunk * ROWS, ROWS), ROWS)
            value = u[rows, :]
            three = dot(wide(value), halves[:, : 3 * LANES])
            gains[0, rows, :] = three[:, LANES : 2 * LANES]
            gains[1, rows, :] = three[:, 2 * LANES :]
            v[rows, :] = along(lx(0), three[:, :LANES])[0]
            g1, g2, g3, g4 = along(halves[:, 7 * LANES : 7 * LANES + DEPTH], cross(value))
            pair[0, rows, :] = dot(wide(g1), halves[:, 3 * LANES : 4 * LANES])
            pair[1, rows, :] = dot(wide(g2), halves[:, 4 * LANES : 5 * LANES])
            gains[2, rows, :] = g3
            gains[3, rows, :] = g4
            return carry

        lax.fori_loop(0, CHUNKS, first, 0)

        def second(k, carry):
            cuts = [pl.ds(k * GROUP + i, NV, stride=FOLD) for i in range(GROUP)]
            s = dot(lz(0), jnp.concatenate([tall(v[cut, :]) for cut in cuts], axis=1))
            for order, w in (((0, 1, 2, 4), 1), ((3, 5), 2)):
                hats = [
                    tall(s[:, i * LANES : (i + 1) * LANES] * spectrum(f, k * GROUP + i))
                    for f in order
                    for i in range(GROUP)
                ]
                result = dot(lz(w), jnp.concatenate(hats, axis=1))
                for n, f in enumerate(order):
                    for i in range(GROUP):
                        at = (n * GROUP + i) * LANES
                        fields[f, cuts[i], :] = result[:, at : at + LANES]
            for n in range(4):
                value = jnp.concatenate([tall(gains[n, cut, :]) for cut in cuts], axis=1)
                result = dot(lz(3 + n), value)
                for i in range(GROUP):
                    gains[n, cuts[i], :] = result[:, i * LANES : (i + 1) * LANES]
            return carry

        lax.fori_loop(0, FOLD // GROUP, second, 0)

        def third(k, carry):
            chunk = jnp.bitwise_xor(mine, CHUNKS - 1 - k)
            rows = pl.ds(pl.multiple_of(chunk * ROWS, ROWS), ROWS)
            even_x = along(lx(1), jnp.concatenate([fields[f, rows, :] for f in (0, 1, 2, 3)], axis=0))[0]
            odd_x = along(lx(2), jnp.concatenate([fields[f, rows, :] for f in (4, 5)], axis=0))[0]
            even = dot(wide(jnp.concatenate([even_x[: 3 * ROWS], odd_x[ROWS:]], axis=0)), halves[:, 5 * LANES : 6 * LANES])
            odd = dot(wide(jnp.concatenate([even_x[3 * ROWS :], odd_x[:ROWS]], axis=0)), halves[:, 6 * LANES : 7 * LANES])
            value = u[rows, :]
            result = (gains[0, rows, :] - value) * even[:ROWS]
            result += gains[1, rows, :] * odd[:ROWS]
            result += (pair[0, rows, :] - value) * even[ROWS : 2 * ROWS]
            result += pair[1, rows, :] * odd[ROWS:]
            result += (cross(gains[2, rows, :]) - value) * even[2 * ROWS : 3 * ROWS]
            result += cross(gains[3, rows, :]) * even[3 * ROWS :]
            weight = jnp.concatenate([single[SPEC_ROWS : SPEC_ROWS + NV]] * BLOCKS, axis=0)
            term[...] = speed_rate * result + wall * weight * um[rows, :]
            for p in range(per):
                slab = chunk * per + p

                def write(t, tile):
                    sback[c, slab, :, t * LANES : (t + 1) * LANES] = tile

                pack(
                    lambda xl: term[pl.ds(p * planes * FOLD + xl, planes, stride=FOLD), :],
                    write, planes,
                )
                for m in range(nvel):
                    @pl.when(jnp.logical_and(me == m, slab != m))
                    def _():
                        pltpu.make_async_remote_copy(
                            src_ref=sback.at[c, slab], dst_ref=back.at[c, :, m, :],
                            send_sem=out_send.at[c, jnp.bitwise_xor(slab, m)],
                            recv_sem=out_recv.at[c, jnp.bitwise_xor(slab, m)],
                            device_id=(sp, slab), device_id_type=MESH,
                        ).start()

                    @pl.when(jnp.logical_and(me == m, slab == m))
                    def _():
                        pltpu.make_async_copy(
                            sback.at[c, m], back.at[c, :, m, :], own_out.at[c]
                        ).start()
            return carry

        lax.fori_loop(0, CHUNKS, third, 0)
        return carry

    lax.fori_loop(0, own, cell_step, 0)
    for r in range(1, nvel):
        sending(own - 1, me, r, jnp.bitwise_xor(me, r), 0).wait_send()
    for c in range(own):
        for r in range(1, nvel):
            peer = jnp.bitwise_xor(me, r)
            copy = pltpu.make_async_remote_copy(
                src_ref=sback.at[c, peer], dst_ref=back.at[c, :, 0, :],
                send_sem=out_send.at[c, r], recv_sem=out_recv.at[c, r],
                device_id=(sp, peer), device_id_type=MESH,
            )
            copy.wait_send()
            copy.wait_recv()
        pltpu.make_async_copy(sback.at[c, me], back.at[c, :, 0, :], own_out.at[c]).wait()
        cut = slice(c * nvel, (c + 1) * nvel)
        for z in range(planes):
            out[z, cut, :] = out[z, cut, :] + back[c, z]


def solution(mesh):
    nspace, nvel = mesh.shape["space"], mesh.shape["vel"]
    tables = build_tables()

    def body(distribution, collision_rate, face_flags):
        cells, planes, width = distribution.shape
        own = cells // nvel
        size = (NV * FOLD, LANES)
        f32 = jnp.float32
        dma = pltpu.SemaphoreType.DMA
        result = pl.pallas_call(
            functools.partial(step_kernel, nspace, nvel, nspace * cells),
            out_shape=jax.ShapeDtypeStruct((planes, cells, width), f32),
            in_specs=[pl.BlockSpec(memory_space=pltpu.HBM)] * (3 + len(tables)),
            out_specs=pl.BlockSpec(memory_space=pltpu.VMEM),
            scratch_shapes=[
                pltpu.VMEM((planes, cells, width), f32),
                pltpu.VMEM((own, nvel, planes, width), f32),
                pltpu.VMEM((own, nvel, planes, width), f32),
                pltpu.VMEM((own, planes, nvel, width), f32),
                pltpu.VMEM((2, planes, width // 2), f32),
                pltpu.VMEM(size, f32),
                pltpu.VMEM(size, f32),
                pltpu.VMEM(size, f32),
                pltpu.VMEM((4,) + size, f32),
                pltpu.VMEM((2,) + size, f32),
                pltpu.VMEM((6,) + size, f32),
                pltpu.VMEM((ROWS, LANES), f32),
                pltpu.SMEM((cells,), f32),
                pltpu.SMEM((nspace * cells,), jnp.int32),
                *[pltpu.VMEM(t.shape, t.dtype) for t in tables],
                dma((own + 4,)),
                dma((own, nvel)),
                dma((own, nvel)),
                dma((own, nvel)),
                dma((own, nvel)),
                dma((own,)),
                dma((own,)),
                dma((2,)),
                dma((2,)),
            ],
            compiler_params=pltpu.CompilerParams(
                collective_id=0, has_side_effects=True, vmem_limit_bytes=53 * 1024 * 1024
            ),
            cost_estimate=pl.CostEstimate(
                flops=10**9, bytes_accessed=10 * 2**20, transcendentals=0
            ),
        )(
            jnp.transpose(distribution, (1, 0, 2)), collision_rate, face_flags,
            *[jnp.asarray(t) for t in tables],
        )
        return jnp.transpose(result, (1, 0, 2))

    return jax.shard_map(
        body,
        mesh=mesh,
        in_specs=(P("space", "vel", None), P("space"), P()),
        out_specs=P("space", "vel", None),
        check_vma=False,
    )
```

```python
import functools
import math

import jax
import jax.numpy as jnp
import ml_dtypes
import numpy as np
from jax import lax
from jax.experimental import pallas as pl
from jax.experimental.pallas import tpu as pltpu
from jax.sharding import PartitionSpec as P

NV = 48
LENGTH = 8.0
RADIUS = 6.0
COURANT = 0.9
GOLDEN = (1.0 + math.sqrt(5.0)) / 2.0
SCALE = math.sqrt(1.0 + GOLDEN * GOLDEN)
HALF = 64
LANES = 128
FOLD = NV // 2
PLANES = 12
CHUNKS = NV // PLANES
ROWS = PLANES * FOLD
BLOCKS = ROWS // NV
GROUP = 4
BF = jnp.bfloat16
MESH = pl.DeviceIdType.MESH


def real_basis():
    j = np.arange(NV)
    q = np.zeros((NV, NV))
    for f in range(25):
        q[f] = np.cos(2 * np.pi * f * j / NV) * (1.0 if f in (0, 24) else math.sqrt(2.0))
    for f in range(1, 24):
        q[24 + f] = np.sin(2 * np.pi * f * j / NV) * math.sqrt(2.0)
    q /= math.sqrt(NV)
    odd = np.zeros((NV, NV))
    for f in range(1, 24):
        odd[:, f] = -q[24 + f]
        odd[:, 24 + f] = q[f]
    mag = np.concatenate([np.arange(24), [0], np.arange(1, 24)]) * (math.pi / LENGTH)
    return q, odd, mag


def circulants():
    j = np.arange(NV)
    k = np.where(j < 24, j, np.where(j == 24, 0, j - NV))
    xi = k * (math.pi / LENGTH)
    f = np.fft.fft(np.eye(NV), axis=0)

    def real(mult):
        return np.real(np.fft.ifft(mult[:, None] * f, axis=0))

    result = []
    for length in (1.0 / SCALE, GOLDEN / SCALE):
        angle = 0.5 * RADIUS * xi * length
        result.append((real(np.cos(angle)), real(1j * np.sin(angle))))
    return result


def split_np(w):
    w = np.asarray(w, np.float32)
    hi = w.astype(ml_dtypes.bfloat16)
    lo = (w - hi.astype(np.float32)).astype(ml_dtypes.bfloat16)
    return hi, lo


def left(w):
    hi, lo = split_np(w)
    return np.concatenate([hi, hi, lo], axis=1)


def right(blocks):
    full = np.zeros((LANES, LANES))
    for i in range(2):
        for j in range(2):
            full[i * HALF : i * HALF + NV, j * HALF : j * HALF + NV] = blocks[i][j].T
    hi, lo = split_np(full)
    return np.concatenate([hi, hi, lo], axis=0)


def apart(w):
    return right([[w, 0 * w], [0 * w, w]])


def crossed(w):
    return right([[w, w], [w, -w]])


def pair_left(even, odd):
    none = np.zeros((FOLD, FOLD))
    return np.block([[even, none], [none, even], [odd, none], [none, odd]])


def build_tables():
    q, odd, mag = real_basis()
    (c1, d1), (c2, d2) = circulants()
    freq = np.concatenate([np.arange(25), np.arange(1, 24)])
    ie, io = np.where(freq % 2 == 0)[0], np.where(freq % 2 == 1)[0]
    mz, mx, my = mag[:, None, None], mag[None, :, None], mag[None, None, :]
    square = mz * mz + mx * mx + my * my

    def sinc(p):
        return np.sinc(RADIUS * np.sqrt(np.maximum(square - p * p, 0.0)) / (2.0 * math.pi))

    plus, minus = [], []
    for first, second in ((my, mz), (mx, my), (mz, mx)):
        same = sinc((first + GOLDEN * second) / SCALE)
        other = sinc((GOLDEN * second - first) / SCALE)
        plus.append((same + other) / 6.0)
        minus.append((other - same) / 6.0)
    values = np.stack(plus + minus).transpose(0, 2, 1, 3)
    spec = np.zeros((6, FOLD, NV, LANES), np.float32)
    spec[..., :NV] = values[:, ie]
    spec[..., HALF : HALF + NV] = values[:, io]

    def ring(c):
        a, b = c[:FOLD, :FOLD], c[:FOLD, FOLD:]
        return pair_left((a + b) / 2.0, (a - b) / 2.0)

    along_z = np.stack([left(w) for w in (q, q.T, odd, c2, d2, c1, d1)])
    along_x = np.stack(
        [
            left(pair_left(q[ie, :FOLD], q[io, :FOLD])),
            left(pair_left(q.T[:FOLD, ie], q.T[:FOLD, io])),
            left(pair_left(odd[:FOLD, ie], odd[:FOLD, io])),
        ]
    )
    gain_x = left(np.concatenate([ring(c1), ring(d1), ring(c2), ring(d2)], axis=0))
    right_first = np.concatenate([crossed(q), apart(c1), apart(d1)], axis=1)
    right_rest = np.stack([crossed(w) for w in (c2, d2, q.T, odd)])
    speed = np.abs(COURANT * (np.arange(NV) - (NV - 1) / 2.0) / ((NV - 1) / 2.0))
    fold = np.zeros((FOLD, LANES), np.float32)
    fold[:, :HALF] = speed[:FOLD, None]
    fold[:, HALF:] = speed[FOLD:, None]
    flat = np.broadcast_to(np.repeat(speed, NV), (8, NV * NV)).astype(np.float32)
    single = np.concatenate(
        [
            spec.reshape(-1, LANES),
            np.tile(fold, (2, 1)),
            flat.reshape(8, -1, LANES).transpose(1, 0, 2).reshape(-1, LANES),
        ]
    )

    def padded(w):
        w = w.reshape(-1, w.shape[-1])
        return np.pad(w, ((0, 3 * LANES - w.shape[0]), (0, 2 * LANES - w.shape[1])))

    halves = np.concatenate(
        [right_first, *right_rest, padded(gain_x), padded(along_x), padded(along_z)], axis=1
    )
    return single, halves


SPEC_ROWS = 6 * FOLD * NV
DEPTH = 3 * NV


def parts(x):
    hi = x.astype(BF)
    lo = (x - hi.astype(jnp.float32)).astype(BF)
    return hi, lo


def tall(x):
    hi, lo = parts(x)
    return jnp.concatenate([hi, lo, hi], axis=0)


def wide(x):
    hi, lo = parts(x)
    return jnp.concatenate([hi, lo, hi], axis=1)


def dot(a, b):
    return jnp.dot(a, b, preferred_element_type=jnp.float32)


def lanes_of(rows):
    return lax.broadcasted_iota(jnp.int32, (rows, LANES), 1)


def turn(x, shift):
    shift %= LANES
    return pltpu.roll(x, shift, axis=1) if shift else x


def along(w, x):
    count = x.shape[0] // NV
    result = dot(w, jnp.concatenate([tall(x[i * NV : (i + 1) * NV]) for i in range(count)], axis=1))
    low = lanes_of(NV) < HALF
    fields = []
    for n in range(w.shape[0] // (2 * NV)):
        blocks = []
        for i in range(count):
            both = result[2 * NV * n : 2 * NV * (n + 1), i * LANES : (i + 1) * LANES]
            blocks.append(jnp.where(low, both[:NV], both[NV:]))
        fields.append(jnp.concatenate(blocks, axis=0))
    return fields


def cross(x):
    other = pltpu.roll(x, HALF, axis=1)
    return jnp.where(lanes_of(x.shape[0]) < HALF, other + x, other - x)


def unpack(block, u, um, start, planes):
    lane = lanes_of(planes)
    for xl in range(FOLD):
        tile, offset = divmod(NV * xl, LANES)
        pieces = []
        for side in range(2):
            t = tile + side * (NV * FOLD // LANES)
            piece = block[:, t * LANES : (t + 1) * LANES]
            if offset + NV > LANES:
                piece = jnp.where(lane >= offset, piece, block[:, (t + 1) * LANES : (t + 2) * LANES])
            pieces.append(turn(piece, side * HALF - offset))
        row = jnp.where(lane < HALF, pieces[0], pieces[1])
        u[pl.ds(start + xl, planes, stride=FOLD), :] = row
        um[pl.ds(start + FOLD - 1 - xl, planes, stride=FOLD), :] = turn(row, HALF)


def pack(read, write, planes):
    lane = lanes_of(planes)
    rows = [read(xl) for xl in range(FOLD)]
    for t in range(NV * FOLD // LANES):
        for side in range(2):
            tile = None
            for xl in range(t * LANES // NV, (t * LANES + LANES - 1) // NV + 1):
                offset = NV * xl - t * LANES
                piece = turn(rows[xl], offset - side * HALF)
                tile = piece if tile is None else jnp.where(lane >= offset, piece, tile)
            write(t + side * (NV * FOLD // LANES), tile)


def step_kernel(
    nspace, nvel, total, *refs,
):
    (
        x_hbm, rate_hbm, flags_hbm, single_hbm, halves_hbm, out,
        xv, stage, sback, back, halo, u, um, v, gains, pair, fields, term,
        rate, flags, single, halves,
        load_sem, in_send, in_recv, out_send, out_recv, own_in, own_out, halo_send, halo_recv,
    ) = refs
    planes, cells, width = xv.shape
    own = cells // nvel
    half = width // 2
    per = PLANES // planes
    sp, me = lax.axis_index("space"), lax.axis_index("vel")
    after, before = lax.rem(sp + 1, nspace), lax.rem(sp + nspace - 1, nspace)
    barrier = pltpu.get_barrier_semaphore()

    def load(i, source, target):
        return pltpu.make_async_copy(source, target, load_sem.at[i])

    first_x = [
        load(c, x_hbm.at[:, pl.ds(c * (cells // own), cells // own)], xv.at[:, pl.ds(c * (cells // own), cells // own)])
        for c in range(own)
    ]
    tables = [
        load(own, single_hbm, single),
        load(own + 1, halves_hbm, halves),
        load(own + 2, rate_hbm, rate),
        load(own + 3, flags_hbm, flags),
    ]
    first_x[0].start()
    for r in range(1, nvel):
        peer = jnp.bitwise_xor(me, r)
        pl.semaphore_signal(barrier, inc=1, device_id=(sp, peer), device_id_type=MESH)
    pl.semaphore_signal(barrier, inc=1, device_id=(after, me), device_id_type=MESH)
    pl.semaphore_signal(barrier, inc=1, device_id=(before, me), device_id_type=MESH)
    pl.semaphore_wait(barrier, nvel + 1)
    first_x[0].wait()

    def sending(c, m, r, peer, row):
        return pltpu.make_async_remote_copy(
            src_ref=xv.at[:, row, :], dst_ref=stage.at[c, m],
            send_sem=in_send.at[c, r], recv_sem=in_recv.at[c, r],
            device_id=(sp, peer), device_id_type=MESH,
        )

    def start_in(c):
        for m in range(nvel):
            @pl.when(me == m)
            def _():
                for r in range(1, nvel):
                    sending(c, m, r, m ^ r, c * nvel + (m ^ r)).start()
                pltpu.make_async_copy(
                    xv.at[:, c * nvel + m, :], stage.at[c, m], own_in.at[c]
                ).start()

    start_in(0)
    for copy in first_x[1:] + tables:
        copy.start()
    for copy in first_x[1:]:
        copy.wait()
    halos = [
        pltpu.make_async_remote_copy(
            src_ref=xv.at[:, cells - 1, pl.ds(half, half)], dst_ref=halo.at[0],
            send_sem=halo_send.at[0], recv_sem=halo_recv.at[0],
            device_id=(after, me), device_id_type=MESH,
        ),
        pltpu.make_async_remote_copy(
            src_ref=xv.at[:, 0, pl.ds(0, half)], dst_ref=halo.at[1],
            send_sem=halo_send.at[1], recv_sem=halo_recv.at[1],
            device_id=(before, me), device_id_type=MESH,
        ),
    ]
    for copy in halos:
        copy.start()
    for copy in tables:
        copy.wait()

    def lower_wall(cell):
        return flags[cell] == 1

    def upper_wall(cell):
        return jnp.logical_or(cell + 1 >= total, flags[jnp.minimum(cell + 1, total - 1)] == 1)

    row_of = lax.broadcasted_iota(jnp.int32, (cells, LANES), 0)
    keep_lower = jnp.zeros((cells, LANES), jnp.float32)
    keep_upper = jnp.zeros((cells, LANES), jnp.float32)
    for c in range(cells):
        cell = sp * cells + c
        low = jnp.where(lower_wall(cell), 0.0, 1.0)
        high = jnp.where(upper_wall(cell), 0.0, 1.0)
        keep_lower = jnp.where(row_of == c, low, keep_lower)
        keep_upper = jnp.where(row_of == c, high, keep_upper)
    at_first = jnp.where(sp == 0, 1.0, 0.0)
    for copy in halos:
        copy.wait()

    for z in range(planes):
        for t in range(width // LANES):
            cut = slice(t * LANES, (t + 1) * LANES)
            value = xv[z, :, cut]
            at = SPEC_ROWS + NV + 8 * t
            weight = jnp.concatenate([single[at : at + 8]] * (cells // 8), axis=0)
            if t >= half // LANES:
                edge = halo[0, z : z + 1, t * LANES - half : (t + 1) * LANES - half]
                edge = edge + at_first * (value[:1] - edge)
                near = jnp.where(row_of == 0, edge, pltpu.roll(value, 1, axis=0))
                keep = keep_lower
            else:
                edge = halo[1, z : z + 1, cut]
                near = jnp.where(row_of == cells - 1, edge, pltpu.roll(value, cells - 1, axis=0))
                keep = keep_upper
            out[z, :, cut] = value - weight * (value - keep * near)

    for c in range(1, own):
        for r in range(1, nvel):
            sending(c - 1, me, r, jnp.bitwise_xor(me, r), 0).wait_send()
        start_in(c)

    low_lanes = lanes_of(1) < HALF
    mine = me // per

    def lx(n):
        return halves[2 * NV * n : 2 * NV * (n + 1), 9 * LANES : 9 * LANES + DEPTH]

    def lz(n):
        return halves[NV * n : NV * (n + 1), 11 * LANES : 11 * LANES + DEPTH]

    def spectrum(f, xl):
        return single[pl.ds(pl.multiple_of((f * FOLD + xl) * NV, NV), NV), :]

    def cell_step(c, carry):
        cell = sp * cells + c * nvel + me
        speed_rate = rate[c * nvel + me]
        wall = jnp.where(
            low_lanes,
            jnp.where(upper_wall(cell), 1.0, 0.0),
            jnp.where(lower_wall(cell), 1.0, 0.0),
        )

        def first(k, carry):
            chunk = jnp.bitwise_xor(mine, k)
            for p in range(per):
                slab = chunk * per + p

                @pl.when(slab != me)
                def _():
                    r = jnp.bitwise_xor(slab, me)
                    sending(c, slab, r, slab, 0).wait_recv()

                @pl.when(slab == me)
                def _():
                    pltpu.make_async_copy(xv.at[:, 0, :], stage.at[c, me], own_in.at[c]).wait()

                unpack(stage.at[c, slab], u, um, slab * (planes * FOLD), planes)
            rows = pl.ds(pl.multiple_of(chunk * ROWS, ROWS), ROWS)
            value = u[rows, :]
            three = dot(wide(value), halves[:, : 3 * LANES])
            gains[0, rows, :] = three[:, LANES : 2 * LANES]
            gains[1, rows, :] = three[:, 2 * LANES :]
            v[rows, :] = along(lx(0), three[:, :LANES])[0]
            g1, g2, g3, g4 = along(halves[:, 7 * LANES : 7 * LANES + DEPTH], cross(value))
            pair[0, rows, :] = dot(wide(g1), halves[:, 3 * LANES : 4 * LANES])
            pair[1, rows, :] = dot(wide(g2), halves[:, 4 * LANES : 5 * LANES])
            gains[2, rows, :] = g3
            gains[3, rows, :] = g4
            return carry

        lax.fori_loop(0, CHUNKS, first, 0)

        def second(k, carry):
            cuts = [pl.ds(k * GROUP + i, NV, stride=FOLD) for i in range(GROUP)]
            s = dot(lz(0), jnp.concatenate([tall(v[cut, :]) for cut in cuts], axis=1))
            for order, w in (((0, 1, 2, 4), 1), ((3, 5), 2)):
                hats = [
                    tall(s[:, i * LANES : (i + 1) * LANES] * spectrum(f, k * GROUP + i))
                    for f in order
                    for i in range(GROUP)
                ]
                result = dot(lz(w), jnp.concatenate(hats, axis=1))
                for n, f in enumerate(order):
                    for i in range(GROUP):
                        at = (n * GROUP + i) * LANES
                        fields[f, cuts[i], :] = result[:, at : at + LANES]
            for n in range(4):
                value = jnp.concatenate([tall(gains[n, cut, :]) for cut in cuts], axis=1)
                result = dot(lz(3 + n), value)
                for i in range(GROUP):
                    gains[n, cuts[i], :] = result[:, i * LANES : (i + 1) * LANES]
            return carry

        lax.fori_loop(0, FOLD // GROUP, second, 0)

        def third(k, carry):
            swap = jnp.logical_and(c == own - 1, k < 2)
            flip = CHUNKS - 1 - k
            chunk = jnp.bitwise_xor(mine, jnp.where(swap, jnp.bitwise_xor(flip, 1), flip))
            rows = pl.ds(pl.multiple_of(chunk * ROWS, ROWS), ROWS)
            even_x = along(lx(1), jnp.concatenate([fields[f, rows, :] for f in (0, 1, 2, 3)], axis=0))[0]
            odd_x = along(lx(2), jnp.concatenate([fields[f, rows, :] for f in (4, 5)], axis=0))[0]
            even = dot(wide(jnp.concatenate([even_x[: 3 * ROWS], odd_x[ROWS:]], axis=0)), halves[:, 5 * LANES : 6 * LANES])
            odd = dot(wide(jnp.concatenate([even_x[3 * ROWS :], odd_x[:ROWS]], axis=0)), halves[:, 6 * LANES : 7 * LANES])
            value = u[rows, :]
            result = (gains[0, rows, :] - value) * even[:ROWS]
            result += gains[1, rows, :] * odd[:ROWS]
            result += (pair[0, rows, :] - value) * even[ROWS : 2 * ROWS]
            result += pair[1, rows, :] * odd[ROWS:]
            result += (cross(gains[2, rows, :]) - value) * even[2 * ROWS : 3 * ROWS]
            result += cross(gains[3, rows, :]) * even[3 * ROWS :]
            weight = jnp.concatenate([single[SPEC_ROWS : SPEC_ROWS + NV]] * BLOCKS, axis=0)
            term[...] = speed_rate * result + wall * weight * um[rows, :]
            for p in range(per):
                slab = chunk * per + p

                def write(t, tile):
                    sback[c, slab, :, t * LANES : (t + 1) * LANES] = tile

                pack(
                    lambda xl: term[pl.ds(p * planes * FOLD + xl, planes, stride=FOLD), :],
                    write, planes,
                )
                for m in range(nvel):
                    @pl.when(jnp.logical_and(me == m, slab != m))
                    def _():
                        pltpu.make_async_remote_copy(
                            src_ref=sback.at[c, slab], dst_ref=back.at[c, :, m, :],
                            send_sem=out_send.at[c, jnp.bitwise_xor(slab, m)],
                            recv_sem=out_recv.at[c, jnp.bitwise_xor(slab, m)],
                            device_id=(sp, slab), device_id_type=MESH,
                        ).start()

                    @pl.when(jnp.logical_and(me == m, slab == m))
                    def _():
                        pltpu.make_async_copy(
                            sback.at[c, m], back.at[c, :, m, :], own_out.at[c]
                        ).start()
            return carry

        lax.fori_loop(0, CHUNKS, third, 0)
        return carry

    lax.fori_loop(0, own, cell_step, 0)
    for r in range(1, nvel):
        sending(own - 1, me, r, jnp.bitwise_xor(me, r), 0).wait_send()
    for c in range(own):
        for r in range(1, nvel):
            peer = jnp.bitwise_xor(me, r)
            copy = pltpu.make_async_remote_copy(
                src_ref=sback.at[c, peer], dst_ref=back.at[c, :, 0, :],
                send_sem=out_send.at[c, r], recv_sem=out_recv.at[c, r],
                device_id=(sp, peer), device_id_type=MESH,
            )
            copy.wait_send()
            copy.wait_recv()
        pltpu.make_async_copy(sback.at[c, me], back.at[c, :, 0, :], own_out.at[c]).wait()
        cut = slice(c * nvel, (c + 1) * nvel)
        for z in range(planes):
            out[z, cut, :] = out[z, cut, :] + back[c, z]


def solution(mesh):
    nspace, nvel = mesh.shape["space"], mesh.shape["vel"]
    tables = build_tables()

    def body(distribution, collision_rate, face_flags):
        cells, planes, width = distribution.shape
        own = cells // nvel
        size = (NV * FOLD, LANES)
        f32 = jnp.float32
        dma = pltpu.SemaphoreType.DMA
        result = pl.pallas_call(
            functools.partial(step_kernel, nspace, nvel, nspace * cells),
            out_shape=jax.ShapeDtypeStruct((planes, cells, width), f32),
            in_specs=[pl.BlockSpec(memory_space=pltpu.HBM)] * (3 + len(tables)),
            out_specs=pl.BlockSpec(memory_space=pltpu.VMEM),
            scratch_shapes=[
                pltpu.VMEM((planes, cells, width), f32),
                pltpu.VMEM((own, nvel, planes, width), f32),
                pltpu.VMEM((own, nvel, planes, width), f32),
                pltpu.VMEM((own, planes, nvel, width), f32),
                pltpu.VMEM((2, planes, width // 2), f32),
                pltpu.VMEM(size, f32),
                pltpu.VMEM(size, f32),
                pltpu.VMEM(size, f32),
                pltpu.VMEM((4,) + size, f32),
                pltpu.VMEM((2,) + size, f32),
                pltpu.VMEM((6,) + size, f32),
                pltpu.VMEM((ROWS, LANES), f32),
                pltpu.SMEM((cells,), f32),
                pltpu.SMEM((nspace * cells,), jnp.int32),
                *[pltpu.VMEM(t.shape, t.dtype) for t in tables],
                dma((own + 4,)),
                dma((own, nvel)),
                dma((own, nvel)),
                dma((own, nvel)),
                dma((own, nvel)),
                dma((own,)),
                dma((own,)),
                dma((2,)),
                dma((2,)),
            ],
            compiler_params=pltpu.CompilerParams(
                collective_id=0, has_side_effects=True, vmem_limit_bytes=53 * 1024 * 1024
            ),
            cost_estimate=pl.CostEstimate(
                flops=10**9, bytes_accessed=10 * 2**20, transcendentals=0
            ),
        )(
            jnp.transpose(distribution, (1, 0, 2)), collision_rate, face_flags,
            *[jnp.asarray(t) for t in tables],
        )
        return jnp.transpose(result, (1, 0, 2))

    return jax.shard_map(
        body,
        mesh=mesh,
        in_specs=(P("space", "vel", None), P("space"), P()),
        out_specs=P("space", "vel", None),
        check_vma=False,
    )
```

```python
import functools
import math

import jax
import jax.numpy as jnp
import ml_dtypes
import numpy as np
from jax import lax
from jax.experimental import pallas as pl
from jax.experimental.pallas import tpu as pltpu
from jax.sharding import PartitionSpec as P

NV = 48
LENGTH = 8.0
RADIUS = 6.0
COURANT = 0.9
GOLDEN = (1.0 + math.sqrt(5.0)) / 2.0
SCALE = math.sqrt(1.0 + GOLDEN * GOLDEN)
HALF = 64
LANES = 128
FOLD = NV // 2
PLANES = 12
CHUNKS = NV // PLANES
ROWS = PLANES * FOLD
BLOCKS = ROWS // NV
GROUP = 4
BF = jnp.bfloat16
MESH = pl.DeviceIdType.MESH


def real_basis():
    j = np.arange(NV)
    q = np.zeros((NV, NV))
    for f in range(25):
        q[f] = np.cos(2 * np.pi * f * j / NV) * (1.0 if f in (0, 24) else math.sqrt(2.0))
    for f in range(1, 24):
        q[24 + f] = np.sin(2 * np.pi * f * j / NV) * math.sqrt(2.0)
    q /= math.sqrt(NV)
    odd = np.zeros((NV, NV))
    for f in range(1, 24):
        odd[:, f] = -q[24 + f]
        odd[:, 24 + f] = q[f]
    mag = np.concatenate([np.arange(24), [0], np.arange(1, 24)]) * (math.pi / LENGTH)
    return q, odd, mag


def circulants():
    j = np.arange(NV)
    k = np.where(j < 24, j, np.where(j == 24, 0, j - NV))
    xi = k * (math.pi / LENGTH)
    f = np.fft.fft(np.eye(NV), axis=0)

    def real(mult):
        return np.real(np.fft.ifft(mult[:, None] * f, axis=0))

    result = []
    for length in (1.0 / SCALE, GOLDEN / SCALE):
        angle = 0.5 * RADIUS * xi * length
        result.append((real(np.cos(angle)), real(1j * np.sin(angle))))
    return result


def split_np(w):
    w = np.asarray(w, np.float32)
    hi = w.astype(ml_dtypes.bfloat16)
    lo = (w - hi.astype(np.float32)).astype(ml_dtypes.bfloat16)
    return hi, lo


def left(w):
    hi, lo = split_np(w)
    return np.concatenate([hi, hi, lo], axis=1)


def right(blocks):
    full = np.zeros((LANES, LANES))
    for i in range(2):
        for j in range(2):
            full[i * HALF : i * HALF + NV, j * HALF : j * HALF + NV] = blocks[i][j].T
    hi, lo = split_np(full)
    return np.concatenate([hi, hi, lo], axis=0)


def apart(w):
    return right([[w, 0 * w], [0 * w, w]])


def crossed(w):
    return right([[w, w], [w, -w]])


def pair_left(even, odd):
    none = np.zeros((FOLD, FOLD))
    return np.block([[even, none], [none, even], [odd, none], [none, odd]])


def build_tables():
    q, odd, mag = real_basis()
    (c1, d1), (c2, d2) = circulants()
    freq = np.concatenate([np.arange(25), np.arange(1, 24)])
    ie, io = np.where(freq % 2 == 0)[0], np.where(freq % 2 == 1)[0]
    mz, mx, my = mag[:, None, None], mag[None, :, None], mag[None, None, :]
    square = mz * mz + mx * mx + my * my

    def sinc(p):
        return np.sinc(RADIUS * np.sqrt(np.maximum(square - p * p, 0.0)) / (2.0 * math.pi))

    plus, minus = [], []
    for first, second in ((my, mz), (mx, my), (mz, mx)):
        same = sinc((first + GOLDEN * second) / SCALE)
        other = sinc((GOLDEN * second - first) / SCALE)
        plus.append((same + other) / 6.0)
        minus.append((other - same) / 6.0)
    values = np.stack(plus + minus).transpose(0, 2, 1, 3)
    spec = np.zeros((6, FOLD, NV, LANES), np.float32)
    spec[..., :NV] = values[:, ie]
    spec[..., HALF : HALF + NV] = values[:, io]

    def ring(c):
        a, b = c[:FOLD, :FOLD], c[:FOLD, FOLD:]
        return pair_left((a + b) / 2.0, (a - b) / 2.0)

    along_z = np.stack([left(w) for w in (q, q.T, odd, c2, d2, c1, d1)])
    along_x = np.stack(
        [
            left(pair_left(q[ie, :FOLD], q[io, :FOLD])),
            left(pair_left(q.T[:FOLD, ie], q.T[:FOLD, io])),
            left(pair_left(odd[:FOLD, ie], odd[:FOLD, io])),
        ]
    )
    gain_x = left(np.concatenate([ring(c1), ring(d1), ring(c2), ring(d2)], axis=0))
    right_first = np.concatenate([crossed(q), apart(c1), apart(d1)], axis=1)
    right_rest = np.stack([crossed(w) for w in (c2, d2, q.T, odd)])
    speed = np.abs(COURANT * (np.arange(NV) - (NV - 1) / 2.0) / ((NV - 1) / 2.0))
    fold = np.zeros((FOLD, LANES), np.float32)
    fold[:, :HALF] = speed[:FOLD, None]
    fold[:, HALF:] = speed[FOLD:, None]
    flat = np.broadcast_to(np.repeat(speed, NV), (8, NV * NV)).astype(np.float32)
    single = np.concatenate(
        [
            spec.reshape(-1, LANES),
            np.tile(fold, (2, 1)),
            flat.reshape(8, -1, LANES).transpose(1, 0, 2).reshape(-1, LANES),
        ]
    )

    def padded(w):
        w = w.reshape(-1, w.shape[-1])
        return np.pad(w, ((0, 3 * LANES - w.shape[0]), (0, 2 * LANES - w.shape[1])))

    halves = np.concatenate(
        [right_first, *right_rest, padded(gain_x), padded(along_x), padded(along_z)], axis=1
    )
    return single, halves


SPEC_ROWS = 6 * FOLD * NV
DEPTH = 3 * NV


def parts(x):
    hi = x.astype(BF)
    lo = (x - hi.astype(jnp.float32)).astype(BF)
    return hi, lo


def tall(x):
    hi, lo = parts(x)
    return jnp.concatenate([hi, lo, hi], axis=0)


def wide(x):
    hi, lo = parts(x)
    return jnp.concatenate([hi, lo, hi], axis=1)


def dot(a, b):
    return jnp.dot(a, b, preferred_element_type=jnp.float32)


def lanes_of(rows):
    return lax.broadcasted_iota(jnp.int32, (rows, LANES), 1)


def turn(x, shift):
    shift %= LANES
    return pltpu.roll(x, shift, axis=1) if shift else x


def along(w, x):
    count = x.shape[0] // NV
    result = dot(w, jnp.concatenate([tall(x[i * NV : (i + 1) * NV]) for i in range(count)], axis=1))
    low = lanes_of(NV) < HALF
    fields = []
    for n in range(w.shape[0] // (2 * NV)):
        blocks = []
        for i in range(count):
            both = result[2 * NV * n : 2 * NV * (n + 1), i * LANES : (i + 1) * LANES]
            blocks.append(jnp.where(low, both[:NV], both[NV:]))
        fields.append(jnp.concatenate(blocks, axis=0))
    return fields


def cross(x):
    other = pltpu.roll(x, HALF, axis=1)
    return jnp.where(lanes_of(x.shape[0]) < HALF, other + x, other - x)


def unpack(block, u, um, start, planes):
    lane = lanes_of(planes)
    for xl in range(FOLD):
        tile, offset = divmod(NV * xl, LANES)
        pieces = []
        for side in range(2):
            t = tile + side * (NV * FOLD // LANES)
            piece = block[:, t * LANES : (t + 1) * LANES]
            if offset + NV > LANES:
                piece = jnp.where(lane >= offset, piece, block[:, (t + 1) * LANES : (t + 2) * LANES])
            pieces.append(turn(piece, side * HALF - offset))
        row = jnp.where(lane < HALF, pieces[0], pieces[1])
        u[pl.ds(start + xl, planes, stride=FOLD), :] = row
        um[pl.ds(start + FOLD - 1 - xl, planes, stride=FOLD), :] = turn(row, HALF)


def pack(read, write, planes):
    lane = lanes_of(planes)
    rows = [read(xl) for xl in range(FOLD)]
    for t in range(NV * FOLD // LANES):
        for side in range(2):
            tile = None
            for xl in range(t * LANES // NV, (t * LANES + LANES - 1) // NV + 1):
                offset = NV * xl - t * LANES
                piece = turn(rows[xl], offset - side * HALF)
                tile = piece if tile is None else jnp.where(lane >= offset, piece, tile)
            write(t + side * (NV * FOLD // LANES), tile)


def step_kernel(
    nspace, nvel, total, *refs,
):
    (
        x_hbm, rate_hbm, flags_hbm, single_hbm, halves_hbm, out,
        xv, stage, sback, back, halo, u, um, v, gains, pair, fields, term,
        rate, flags, single, halves,
        load_sem, in_send, in_recv, out_send, out_recv, own_in, own_out, halo_send, halo_recv,
    ) = refs
    planes, cells, width = xv.shape
    own = cells // nvel
    half = width // 2
    per = PLANES // planes
    sp, me = lax.axis_index("space"), lax.axis_index("vel")
    after, before = lax.rem(sp + 1, nspace), lax.rem(sp + nspace - 1, nspace)
    barrier = pltpu.get_barrier_semaphore()

    def load(i, source, target):
        return pltpu.make_async_copy(source, target, load_sem.at[i])

    first_x = [
        load(c, x_hbm.at[:, pl.ds(c * (cells // own), cells // own)], xv.at[:, pl.ds(c * (cells // own), cells // own)])
        for c in range(own)
    ]
    tables = [
        load(own, single_hbm, single),
        load(own + 1, halves_hbm, halves),
        load(own + 2, rate_hbm, rate),
        load(own + 3, flags_hbm, flags),
    ]
    first_x[0].start()
    for r in range(1, nvel):
        peer = jnp.bitwise_xor(me, r)
        pl.semaphore_signal(barrier, inc=1, device_id=(sp, peer), device_id_type=MESH)
    pl.semaphore_signal(barrier, inc=1, device_id=(after, me), device_id_type=MESH)
    pl.semaphore_signal(barrier, inc=1, device_id=(before, me), device_id_type=MESH)
    pl.semaphore_wait(barrier, nvel + 1)
    first_x[0].wait()

    def sending(c, m, r, peer, row):
        return pltpu.make_async_remote_copy(
            src_ref=xv.at[:, row, :], dst_ref=stage.at[c, m],
            send_sem=in_send.at[c, r], recv_sem=in_recv.at[c, r],
            device_id=(sp, peer), device_id_type=MESH,
        )

    def start_in(c):
        for m in range(nvel):
            @pl.when(me == m)
            def _():
                for r in range(1, nvel):
                    sending(c, m, r, m ^ r, c * nvel + (m ^ r)).start()
                pltpu.make_async_copy(
                    xv.at[:, c * nvel + m, :], stage.at[c, m], own_in.at[c]
                ).start()

    start_in(0)
    for copy in first_x[1:] + tables:
        copy.start()
    for copy in first_x[1:]:
        copy.wait()
    halos = [
        pltpu.make_async_remote_copy(
            src_ref=xv.at[:, cells - 1, pl.ds(half, half)], dst_ref=halo.at[0],
            send_sem=halo_send.at[0], recv_sem=halo_recv.at[0],
            device_id=(after, me), device_id_type=MESH,
        ),
        pltpu.make_async_remote_copy(
            src_ref=xv.at[:, 0, pl.ds(0, half)], dst_ref=halo.at[1],
            send_sem=halo_send.at[1], recv_sem=halo_recv.at[1],
            device_id=(before, me), device_id_type=MESH,
        ),
    ]
    for copy in halos:
        copy.start()
    for copy in tables:
        copy.wait()

    def lower_wall(cell):
        return flags[cell] == 1

    def upper_wall(cell):
        return jnp.logical_or(cell + 1 >= total, flags[jnp.minimum(cell + 1, total - 1)] == 1)

    row_of = lax.broadcasted_iota(jnp.int32, (cells, LANES), 0)
    keep_lower = jnp.zeros((cells, LANES), jnp.float32)
    keep_upper = jnp.zeros((cells, LANES), jnp.float32)
    for c in range(cells):
        cell = sp * cells + c
        low = jnp.where(lower_wall(cell), 0.0, 1.0)
        high = jnp.where(upper_wall(cell), 0.0, 1.0)
        keep_lower = jnp.where(row_of == c, low, keep_lower)
        keep_upper = jnp.where(row_of == c, high, keep_upper)
    at_first = jnp.where(sp == 0, 1.0, 0.0)
    for copy in halos:
        copy.wait()

    for z in range(planes):
        for t in range(width // LANES):
            cut = slice(t * LANES, (t + 1) * LANES)
            value = xv[z, :, cut]
            at = SPEC_ROWS + NV + 8 * t
            weight = jnp.concatenate([single[at : at + 8]] * (cells // 8), axis=0)
            if t >= half // LANES:
                edge = halo[0, z : z + 1, t * LANES - half : (t + 1) * LANES - half]
                edge = edge + at_first * (value[:1] - edge)
                near = jnp.where(row_of == 0, edge, pltpu.roll(value, 1, axis=0))
                keep = keep_lower
            else:
                edge = halo[1, z : z + 1, cut]
                near = jnp.where(row_of == cells - 1, edge, pltpu.roll(value, cells - 1, axis=0))
                keep = keep_upper
            out[z, :, cut] = value - weight * (value - keep * near)

    for c in range(1, own):
        for r in range(1, nvel):
            sending(c - 1, me, r, jnp.bitwise_xor(me, r), 0).wait_send()
        start_in(c)

    low_lanes = lanes_of(1) < HALF
    mine = me // per

    def lx(n):
        return halves[2 * NV * n : 2 * NV * (n + 1), 9 * LANES : 9 * LANES + DEPTH]

    def lz(n):
        return halves[NV * n : NV * (n + 1), 11 * LANES : 11 * LANES + DEPTH]

    def spectrum(f, xl):
        return single[pl.ds(pl.multiple_of((f * FOLD + xl) * NV, NV), NV), :]

    def cell_step(c, carry):
        cell = sp * cells + c * nvel + me
        speed_rate = rate[c * nvel + me]
        wall = jnp.where(
            low_lanes,
            jnp.where(upper_wall(cell), 1.0, 0.0),
            jnp.where(lower_wall(cell), 1.0, 0.0),
        )

        def first(k, carry):
            chunk = jnp.bitwise_xor(mine, k)
            for p in range(per):
                slab = chunk * per + p

                @pl.when(slab != me)
                def _():
                    r = jnp.bitwise_xor(slab, me)
                    sending(c, slab, r, slab, 0).wait_recv()

                @pl.when(slab == me)
                def _():
                    pltpu.make_async_copy(xv.at[:, 0, :], stage.at[c, me], own_in.at[c]).wait()

                unpack(stage.at[c, slab], u, um, slab * (planes * FOLD), planes)
            rows = pl.ds(pl.multiple_of(chunk * ROWS, ROWS), ROWS)
            value = u[rows, :]
            three = dot(wide(value), halves[:, : 3 * LANES])
            gains[0, rows, :] = three[:, LANES : 2 * LANES]
            gains[1, rows, :] = three[:, 2 * LANES :]
            v[rows, :] = along(lx(0), three[:, :LANES])[0]
            g1, g2, g3, g4 = along(halves[:, 7 * LANES : 7 * LANES + DEPTH], cross(value))
            pair[0, rows, :] = dot(wide(g1), halves[:, 3 * LANES : 4 * LANES])
            pair[1, rows, :] = dot(wide(g2), halves[:, 4 * LANES : 5 * LANES])
            gains[2, rows, :] = g3
            gains[3, rows, :] = g4
            return carry

        lax.fori_loop(0, CHUNKS, first, 0)

        def second(k, carry):
            cuts = [pl.ds(k * GROUP + i, NV, stride=FOLD) for i in range(GROUP)]
            s = dot(lz(0), jnp.concatenate([tall(v[cut, :]) for cut in cuts], axis=1))
            for order, w in (((0, 1, 2, 4), 1), ((3, 5), 2)):
                hats = [
                    tall(s[:, i * LANES : (i + 1) * LANES] * spectrum(f, k * GROUP + i))
                    for f in order
                    for i in range(GROUP)
                ]
                result = dot(lz(w), jnp.concatenate(hats, axis=1))
                for n, f in enumerate(order):
                    for i in range(GROUP):
                        at = (n * GROUP + i) * LANES
                        fields[f, cuts[i], :] = result[:, at : at + LANES]
            for n in range(4):
                value = jnp.concatenate([tall(gains[n, cut, :]) for cut in cuts], axis=1)
                result = dot(lz(3 + n), value)
                for i in range(GROUP):
                    gains[n, cuts[i], :] = result[:, i * LANES : (i + 1) * LANES]
            return carry

        lax.fori_loop(0, FOLD // GROUP, second, 0)

        def third(k, carry):
            swap = jnp.logical_and(c == own - 1, k < 2)
            flip = CHUNKS - 1 - k
            chunk = jnp.bitwise_xor(mine, jnp.where(swap, jnp.bitwise_xor(flip, 1), flip))
            rows = pl.ds(pl.multiple_of(chunk * ROWS, ROWS), ROWS)
            even_x = along(lx(1), jnp.concatenate([fields[f, rows, :] for f in (0, 1, 2, 3)], axis=0))[0]
            odd_x = along(lx(2), jnp.concatenate([fields[f, rows, :] for f in (4, 5)], axis=0))[0]
            even = dot(wide(jnp.concatenate([even_x[: 3 * ROWS], odd_x[ROWS:]], axis=0)), halves[:, 5 * LANES : 6 * LANES])
            odd = dot(wide(jnp.concatenate([even_x[3 * ROWS :], odd_x[:ROWS]], axis=0)), halves[:, 6 * LANES : 7 * LANES])
            value = u[rows, :]
            result = (gains[0, rows, :] - value) * even[:ROWS]
            result += gains[1, rows, :] * odd[:ROWS]
            result += (pair[0, rows, :] - value) * even[ROWS : 2 * ROWS]
            result += pair[1, rows, :] * odd[ROWS:]
            result += (cross(gains[2, rows, :]) - value) * even[2 * ROWS : 3 * ROWS]
            result += cross(gains[3, rows, :]) * even[3 * ROWS :]
            weight = jnp.concatenate([single[SPEC_ROWS : SPEC_ROWS + NV]] * BLOCKS, axis=0)
            term[:ROWS] = speed_rate * result + wall * weight * um[rows, :]
            for p in range(per):
                slab = chunk * per + p

                def write(t, tile):
                    sback[c, slab, :, t * LANES : (t + 1) * LANES] = tile

                pack(
                    lambda xl: term[pl.ds(p * planes * FOLD + xl, planes, stride=FOLD), :],
                    write, planes,
                )
                for m in range(nvel):
                    @pl.when(jnp.logical_and(me == m, slab != m))
                    def _():
                        pltpu.make_async_remote_copy(
                            src_ref=sback.at[c, slab], dst_ref=back.at[c, :, m, :],
                            send_sem=out_send.at[c, jnp.bitwise_xor(slab, m)],
                            recv_sem=out_recv.at[c, jnp.bitwise_xor(slab, m)],
                            device_id=(sp, slab), device_id_type=MESH,
                        ).start()

                    @pl.when(jnp.logical_and(me == m, slab == m))
                    def _():
                        pltpu.make_async_copy(
                            sback.at[c, m], back.at[c, :, m, :], own_out.at[c]
                        ).start()
            return carry

        lax.fori_loop(0, CHUNKS, third, 0)
        return carry

    lax.fori_loop(0, own, cell_step, 0)
    for r in range(1, nvel):
        sending(own - 1, me, r, jnp.bitwise_xor(me, r), 0).wait_send()
    for c in range(own):
        for r in range(1, nvel):
            peer = jnp.bitwise_xor(me, r)
            copy = pltpu.make_async_remote_copy(
                src_ref=sback.at[c, peer], dst_ref=back.at[c, :, 0, :],
                send_sem=out_send.at[c, r], recv_sem=out_recv.at[c, r],
                device_id=(sp, peer), device_id_type=MESH,
            )
            copy.wait_send()
            copy.wait_recv()
        pltpu.make_async_copy(sback.at[c, me], back.at[c, :, 0, :], own_out.at[c]).wait()
        cut = slice(c * nvel, (c + 1) * nvel)
        for z in range(planes):
            out[z, cut, :] = out[z, cut, :] + back[c, z]


def solution(mesh):
    nspace, nvel = mesh.shape["space"], mesh.shape["vel"]
    tables = build_tables()

    def body(distribution, collision_rate, face_flags):
        cells, planes, width = distribution.shape
        own = cells // nvel
        size = (NV * FOLD, LANES)
        spare = 8 * FOLD
        f32 = jnp.float32
        dma = pltpu.SemaphoreType.DMA
        result = pl.pallas_call(
            functools.partial(step_kernel, nspace, nvel, nspace * cells),
            out_shape=jax.ShapeDtypeStruct((planes, cells, width), f32),
            in_specs=[pl.BlockSpec(memory_space=pltpu.HBM)] * (3 + len(tables)),
            out_specs=pl.BlockSpec(memory_space=pltpu.VMEM),
            scratch_shapes=[
                pltpu.VMEM((planes, cells, width), f32),
                pltpu.VMEM((own, nvel, planes, width), f32),
                pltpu.VMEM((own, nvel, planes, width), f32),
                pltpu.VMEM((own, planes, nvel, width), f32),
                pltpu.VMEM((2, planes, width // 2), f32),
                pltpu.VMEM((NV * FOLD + spare, LANES), f32),
                pltpu.VMEM((NV * FOLD + spare, LANES), f32),
                pltpu.VMEM(size, f32),
                pltpu.VMEM((4,) + size, f32),
                pltpu.VMEM((2,) + size, f32),
                pltpu.VMEM((6,) + size, f32),
                pltpu.VMEM((ROWS + spare, LANES), f32),
                pltpu.SMEM((cells,), f32),
                pltpu.SMEM((nspace * cells,), jnp.int32),
                *[pltpu.VMEM(t.shape, t.dtype) for t in tables],
                dma((own + 4,)),
                dma((own, nvel)),
                dma((own, nvel)),
                dma((own, nvel)),
                dma((own, nvel)),
                dma((own,)),
                dma((own,)),
                dma((2,)),
                dma((2,)),
            ],
            compiler_params=pltpu.CompilerParams(
                collective_id=0, has_side_effects=True, vmem_limit_bytes=53 * 1024 * 1024
            ),
            cost_estimate=pl.CostEstimate(
                flops=10**9, bytes_accessed=10 * 2**20, transcendentals=0
            ),
        )(
            jnp.transpose(distribution, (1, 0, 2)), collision_rate, face_flags,
            *[jnp.asarray(t) for t in tables],
        )
        return jnp.transpose(result, (1, 0, 2))

    return jax.shard_map(
        body,
        mesh=mesh,
        in_specs=(P("space", "vel", None), P("space"), P()),
        out_specs=P("space", "vel", None),
        check_vma=False,
    )
```

```python
import functools
import math

import jax
import jax.numpy as jnp
import ml_dtypes
import numpy as np
from jax import lax
from jax.experimental import pallas as pl
from jax.experimental.pallas import tpu as pltpu
from jax.sharding import PartitionSpec as P

NV = 48
LENGTH = 8.0
RADIUS = 6.0
COURANT = 0.9
GOLDEN = (1.0 + math.sqrt(5.0)) / 2.0
SCALE = math.sqrt(1.0 + GOLDEN * GOLDEN)
HALF = 64
LANES = 128
FOLD = NV // 2
PLANES = 12
CHUNKS = NV // PLANES
ROWS = PLANES * FOLD
BLOCKS = ROWS // NV
GROUP = 4
BF = jnp.bfloat16
MESH = pl.DeviceIdType.MESH


def real_basis():
    j = np.arange(NV)
    q = np.zeros((NV, NV))
    for f in range(25):
        q[f] = np.cos(2 * np.pi * f * j / NV) * (1.0 if f in (0, 24) else math.sqrt(2.0))
    for f in range(1, 24):
        q[24 + f] = np.sin(2 * np.pi * f * j / NV) * math.sqrt(2.0)
    q /= math.sqrt(NV)
    odd = np.zeros((NV, NV))
    for f in range(1, 24):
        odd[:, f] = -q[24 + f]
        odd[:, 24 + f] = q[f]
    mag = np.concatenate([np.arange(24), [0], np.arange(1, 24)]) * (math.pi / LENGTH)
    return q, odd, mag


def circulants():
    j = np.arange(NV)
    k = np.where(j < 24, j, np.where(j == 24, 0, j - NV))
    xi = k * (math.pi / LENGTH)
    f = np.fft.fft(np.eye(NV), axis=0)

    def real(mult):
        return np.real(np.fft.ifft(mult[:, None] * f, axis=0))

    result = []
    for length in (1.0 / SCALE, GOLDEN / SCALE):
        angle = 0.5 * RADIUS * xi * length
        result.append((real(np.cos(angle)), real(1j * np.sin(angle))))
    return result


def split_np(w):
    w = np.asarray(w, np.float32)
    hi = w.astype(ml_dtypes.bfloat16)
    lo = (w - hi.astype(np.float32)).astype(ml_dtypes.bfloat16)
    return hi, lo


def left(w):
    hi, lo = split_np(w)
    return np.concatenate([hi, hi, lo], axis=1)


def right(blocks):
    full = np.zeros((LANES, LANES))
    for i in range(2):
        for j in range(2):
            full[i * HALF : i * HALF + NV, j * HALF : j * HALF + NV] = blocks[i][j].T
    hi, lo = split_np(full)
    return np.concatenate([hi, hi, lo], axis=0)


def apart(w):
    return right([[w, 0 * w], [0 * w, w]])


def crossed(w):
    return right([[w, w], [w, -w]])


def pair_left(even, odd):
    none = np.zeros((FOLD, FOLD))
    return np.block([[even, none], [none, even], [odd, none], [none, odd]])


def build_tables():
    q, odd, mag = real_basis()
    (c1, d1), (c2, d2) = circulants()
    freq = np.concatenate([np.arange(25), np.arange(1, 24)])
    ie, io = np.where(freq % 2 == 0)[0], np.where(freq % 2 == 1)[0]
    mz, mx, my = mag[:, None, None], mag[None, :, None], mag[None, None, :]
    square = mz * mz + mx * mx + my * my

    def sinc(p):
        return np.sinc(RADIUS * np.sqrt(np.maximum(square - p * p, 0.0)) / (2.0 * math.pi))

    plus, minus = [], []
    for first, second in ((my, mz), (mx, my), (mz, mx)):
        same = sinc((first + GOLDEN * second) / SCALE)
        other = sinc((GOLDEN * second - first) / SCALE)
        plus.append((same + other) / 6.0)
        minus.append((other - same) / 6.0)
    values = np.stack(plus + minus).transpose(0, 2, 1, 3)
    spec = np.zeros((6, FOLD, NV, LANES), np.float32)
    spec[..., :NV] = values[:, ie]
    spec[..., HALF : HALF + NV] = values[:, io]

    def ring(c):
        a, b = c[:FOLD, :FOLD], c[:FOLD, FOLD:]
        return pair_left((a + b) / 2.0, (a - b) / 2.0)

    along_z = np.stack([left(w) for w in (q, q.T, odd, c2, d2, c1, d1)])
    along_x = np.stack(
        [
            left(pair_left(q[ie, :FOLD], q[io, :FOLD])),
            left(pair_left(q.T[:FOLD, ie], q.T[:FOLD, io])),
            left(pair_left(odd[:FOLD, ie], odd[:FOLD, io])),
        ]
    )
    gain_x = left(np.concatenate([ring(c1), ring(d1), ring(c2), ring(d2)], axis=0))
    right_first = np.concatenate([crossed(q), apart(c1), apart(d1)], axis=1)
    right_rest = np.stack([crossed(w) for w in (c2, d2, q.T, odd)])
    speed = np.abs(COURANT * (np.arange(NV) - (NV - 1) / 2.0) / ((NV - 1) / 2.0))
    fold = np.zeros((FOLD, LANES), np.float32)
    fold[:, :HALF] = speed[:FOLD, None]
    fold[:, HALF:] = speed[FOLD:, None]
    flat = np.broadcast_to(np.repeat(speed, NV), (8, NV * NV)).astype(np.float32)
    single = np.concatenate(
        [
            spec.reshape(-1, LANES),
            np.tile(fold, (2, 1)),
            flat.reshape(8, -1, LANES).transpose(1, 0, 2).reshape(-1, LANES),
        ]
    )

    def padded(w):
        w = w.reshape(-1, w.shape[-1])
        return np.pad(w, ((0, 3 * LANES - w.shape[0]), (0, 2 * LANES - w.shape[1])))

    halves = np.concatenate(
        [right_first, *right_rest, padded(gain_x), padded(along_x), padded(along_z)], axis=1
    )
    return single, halves


SPEC_ROWS = 6 * FOLD * NV
DEPTH = 3 * NV


def parts(x):
    hi = x.astype(BF)
    lo = (x - hi.astype(jnp.float32)).astype(BF)
    return hi, lo


def tall(x):
    hi, lo = parts(x)
    return jnp.concatenate([hi, lo, hi], axis=0)


def wide(x):
    hi, lo = parts(x)
    return jnp.concatenate([hi, lo, hi], axis=1)


def dot(a, b):
    return jnp.dot(a, b, preferred_element_type=jnp.float32)


def lanes_of(rows):
    return lax.broadcasted_iota(jnp.int32, (rows, LANES), 1)


def turn(x, shift):
    shift %= LANES
    return pltpu.roll(x, shift, axis=1) if shift else x


def along(w, x):
    count = x.shape[0] // NV
    result = dot(w, jnp.concatenate([tall(x[i * NV : (i + 1) * NV]) for i in range(count)], axis=1))
    low = lanes_of(NV) < HALF
    fields = []
    for n in range(w.shape[0] // (2 * NV)):
        blocks = []
        for i in range(count):
            both = result[2 * NV * n : 2 * NV * (n + 1), i * LANES : (i + 1) * LANES]
            blocks.append(jnp.where(low, both[:NV], both[NV:]))
        fields.append(jnp.concatenate(blocks, axis=0))
    return fields


def cross(x):
    other = pltpu.roll(x, HALF, axis=1)
    return jnp.where(lanes_of(x.shape[0]) < HALF, other + x, other - x)


def unpack(block, u, start, planes):
    lane = lanes_of(planes)
    for xl in range(FOLD):
        tile, offset = divmod(NV * xl, LANES)
        pieces = []
        for side in range(2):
            t = tile + side * (NV * FOLD // LANES)
            piece = block[:, t * LANES : (t + 1) * LANES]
            if offset + NV > LANES:
                piece = jnp.where(lane >= offset, piece, block[:, (t + 1) * LANES : (t + 2) * LANES])
            pieces.append(turn(piece, side * HALF - offset))
        row = jnp.where(lane < HALF, pieces[0], pieces[1])
        u[pl.ds(start + xl, planes, stride=FOLD), :] = row


def pack(read, write, planes):
    lane = lanes_of(planes)
    rows = [read(xl) for xl in range(FOLD)]
    for t in range(NV * FOLD // LANES):
        for side in range(2):
            tile = None
            for xl in range(t * LANES // NV, (t * LANES + LANES - 1) // NV + 1):
                offset = NV * xl - t * LANES
                piece = turn(rows[xl], offset - side * HALF)
                tile = piece if tile is None else jnp.where(lane >= offset, piece, tile)
            write(t + side * (NV * FOLD // LANES), tile)


def step_kernel(
    nspace, nvel, total, *refs,
):
    (
        x_hbm, rate_hbm, flags_hbm, single_hbm, halves_hbm, out,
        xv, stage, sback, back, halo, u, v, gains, pair, fields, term,
        rate, flags, single, halves,
        load_sem, in_send, in_recv, out_send, out_recv, own_in, own_out, halo_send, halo_recv,
    ) = refs
    planes, cells, width = xv.shape
    own = cells // nvel
    half = width // 2
    per = PLANES // planes
    sp, me = lax.axis_index("space"), lax.axis_index("vel")
    after, before = lax.rem(sp + 1, nspace), lax.rem(sp + nspace - 1, nspace)
    barrier = pltpu.get_barrier_semaphore()

    def load(i, source, target):
        return pltpu.make_async_copy(source, target, load_sem.at[i])

    first_x = [
        load(c, x_hbm.at[:, pl.ds(c * (cells // own), cells // own)], xv.at[:, pl.ds(c * (cells // own), cells // own)])
        for c in range(own)
    ]
    tables = [
        load(own, single_hbm, single),
        load(own + 1, halves_hbm, halves),
        load(own + 2, rate_hbm, rate),
        load(own + 3, flags_hbm, flags),
    ]
    first_x[0].start()
    for r in range(1, nvel):
        peer = jnp.bitwise_xor(me, r)
        pl.semaphore_signal(barrier, inc=1, device_id=(sp, peer), device_id_type=MESH)
    pl.semaphore_signal(barrier, inc=1, device_id=(after, me), device_id_type=MESH)
    pl.semaphore_signal(barrier, inc=1, device_id=(before, me), device_id_type=MESH)
    pl.semaphore_wait(barrier, nvel + 1)
    first_x[0].wait()

    def sending(c, m, r, peer, row):
        return pltpu.make_async_remote_copy(
            src_ref=xv.at[:, row, :], dst_ref=stage.at[c, m],
            send_sem=in_send.at[c, r], recv_sem=in_recv.at[c, r],
            device_id=(sp, peer), device_id_type=MESH,
        )

    def start_in(c):
        for m in range(nvel):
            @pl.when(me == m)
            def _():
                for r in range(1, nvel):
                    sending(c, m, r, m ^ r, c * nvel + (m ^ r)).start()
                pltpu.make_async_copy(
                    xv.at[:, c * nvel + m, :], stage.at[c, m], own_in.at[c]
                ).start()

    start_in(0)
    for copy in first_x[1:] + tables:
        copy.start()
    for copy in first_x[1:]:
        copy.wait()
    halos = [
        pltpu.make_async_remote_copy(
            src_ref=xv.at[:, cells - 1, pl.ds(half, half)], dst_ref=halo.at[0],
            send_sem=halo_send.at[0], recv_sem=halo_recv.at[0],
            device_id=(after, me), device_id_type=MESH,
        ),
        pltpu.make_async_remote_copy(
            src_ref=xv.at[:, 0, pl.ds(0, half)], dst_ref=halo.at[1],
            send_sem=halo_send.at[1], recv_sem=halo_recv.at[1],
            device_id=(before, me), device_id_type=MESH,
        ),
    ]
    for copy in halos:
        copy.start()
    for copy in tables:
        copy.wait()

    def lower_wall(cell):
        return flags[cell] == 1

    def upper_wall(cell):
        return jnp.logical_or(cell + 1 >= total, flags[jnp.minimum(cell + 1, total - 1)] == 1)

    row_of = lax.broadcasted_iota(jnp.int32, (cells, LANES), 0)
    keep_lower = jnp.zeros((cells, LANES), jnp.float32)
    keep_upper = jnp.zeros((cells, LANES), jnp.float32)
    for c in range(cells):
        cell = sp * cells + c
        low = jnp.where(lower_wall(cell), 0.0, 1.0)
        high = jnp.where(upper_wall(cell), 0.0, 1.0)
        keep_lower = jnp.where(row_of == c, low, keep_lower)
        keep_upper = jnp.where(row_of == c, high, keep_upper)
    at_first = jnp.where(sp == 0, 1.0, 0.0)
    for copy in halos:
        copy.wait()

    for z in range(planes):
        for t in range(width // LANES):
            cut = slice(t * LANES, (t + 1) * LANES)
            value = xv[z, :, cut]
            at = SPEC_ROWS + NV + 8 * t
            weight = jnp.concatenate([single[at : at + 8]] * (cells // 8), axis=0)
            if t >= half // LANES:
                edge = halo[0, z : z + 1, t * LANES - half : (t + 1) * LANES - half]
                edge = edge + at_first * (value[:1] - edge)
                near = jnp.where(row_of == 0, edge, pltpu.roll(value, 1, axis=0))
                keep = keep_lower
            else:
                edge = halo[1, z : z + 1, cut]
                near = jnp.where(row_of == cells - 1, edge, pltpu.roll(value, cells - 1, axis=0))
                keep = keep_upper
            out[z, :, cut] = value - weight * (value - keep * near)

    for c in range(1, own):
        for r in range(1, nvel):
            sending(c - 1, me, r, jnp.bitwise_xor(me, r), 0).wait_send()
        start_in(c)

    low_lanes = lanes_of(1) < HALF
    mine = me // per

    def lx(n):
        return halves[2 * NV * n : 2 * NV * (n + 1), 9 * LANES : 9 * LANES + DEPTH]

    def lz(n):
        return halves[NV * n : NV * (n + 1), 11 * LANES : 11 * LANES + DEPTH]

    def spectrum(f, xl):
        return single[pl.ds(pl.multiple_of((f * FOLD + xl) * NV, NV), NV), :]

    def cell_step(c, carry):
        cell = sp * cells + c * nvel + me
        speed_rate = rate[c * nvel + me]
        wall = jnp.where(
            low_lanes,
            jnp.where(upper_wall(cell), 1.0, 0.0),
            jnp.where(lower_wall(cell), 1.0, 0.0),
        )

        def first(k, carry):
            chunk = jnp.bitwise_xor(mine, k)
            for p in range(per):
                slab = chunk * per + p

                @pl.when(slab != me)
                def _():
                    r = jnp.bitwise_xor(slab, me)
                    sending(c, slab, r, slab, 0).wait_recv()

                @pl.when(slab == me)
                def _():
                    pltpu.make_async_copy(xv.at[:, 0, :], stage.at[c, me], own_in.at[c]).wait()

                unpack(stage.at[c, slab], u, slab * (planes * FOLD), planes)
            rows = pl.ds(pl.multiple_of(chunk * ROWS, ROWS), ROWS)
            value = u[rows, :]
            three = dot(wide(value), halves[:, : 3 * LANES])
            gains[0, rows, :] = three[:, LANES : 2 * LANES]
            gains[1, rows, :] = three[:, 2 * LANES :]
            v[rows, :] = along(lx(0), three[:, :LANES])[0]
            g1, g2, g3, g4 = along(halves[:, 7 * LANES : 7 * LANES + DEPTH], cross(value))
            pair[0, rows, :] = dot(wide(g1), halves[:, 3 * LANES : 4 * LANES])
            pair[1, rows, :] = dot(wide(g2), halves[:, 4 * LANES : 5 * LANES])
            gains[2, rows, :] = g3
            gains[3, rows, :] = g4
            return carry

        lax.fori_loop(0, CHUNKS, first, 0)

        def second(k, carry):
            cuts = [pl.ds(k * GROUP + i, NV, stride=FOLD) for i in range(GROUP)]
            s = dot(lz(0), jnp.concatenate([tall(v[cut, :]) for cut in cuts], axis=1))
            for order, w in (((0, 1, 2, 4), 1), ((3, 5), 2)):
                hats = [
                    tall(s[:, i * LANES : (i + 1) * LANES] * spectrum(f, k * GROUP + i))
                    for f in order
                    for i in range(GROUP)
                ]
                result = dot(lz(w), jnp.concatenate(hats, axis=1))
                for n, f in enumerate(order):
                    for i in range(GROUP):
                        at = (n * GROUP + i) * LANES
                        fields[f, cuts[i], :] = result[:, at : at + LANES]
            for n in range(4):
                value = jnp.concatenate([tall(gains[n, cut, :]) for cut in cuts], axis=1)
                result = dot(lz(3 + n), value)
                for i in range(GROUP):
                    gains[n, cuts[i], :] = result[:, i * LANES : (i + 1) * LANES]
            return carry

        lax.fori_loop(0, FOLD // GROUP, second, 0)

        def third(k, carry):
            swap = jnp.logical_and(c == own - 1, k < 2)
            flip = CHUNKS - 1 - k
            chunk = jnp.bitwise_xor(mine, jnp.where(swap, jnp.bitwise_xor(flip, 1), flip))
            rows = pl.ds(pl.multiple_of(chunk * ROWS, ROWS), ROWS)
            even_x = along(lx(1), jnp.concatenate([fields[f, rows, :] for f in (0, 1, 2, 3)], axis=0))[0]
            odd_x = along(lx(2), jnp.concatenate([fields[f, rows, :] for f in (4, 5)], axis=0))[0]
            even = dot(wide(jnp.concatenate([even_x[: 3 * ROWS], odd_x[ROWS:]], axis=0)), halves[:, 5 * LANES : 6 * LANES])
            odd = dot(wide(jnp.concatenate([even_x[3 * ROWS :], odd_x[:ROWS]], axis=0)), halves[:, 6 * LANES : 7 * LANES])
            value = u[rows, :]
            result = (gains[0, rows, :] - value) * even[:ROWS]
            result += gains[1, rows, :] * odd[:ROWS]
            result += (pair[0, rows, :] - value) * even[ROWS : 2 * ROWS]
            result += pair[1, rows, :] * odd[ROWS:]
            result += (cross(gains[2, rows, :]) - value) * even[2 * ROWS : 3 * ROWS]
            result += cross(gains[3, rows, :]) * even[3 * ROWS :]
            term[:ROWS] = speed_rate * result
            for p in range(per):
                slab = chunk * per + p

                def write(t, tile):
                    sback[c, slab, :, t * LANES : (t + 1) * LANES] = tile

                pack(
                    lambda xl: term[pl.ds(p * planes * FOLD + xl, planes, stride=FOLD), :]
                    + wall * single[SPEC_ROWS + xl : SPEC_ROWS + xl + 1]
                    * turn(u[pl.ds(slab * (planes * FOLD) + FOLD - 1 - xl, planes, stride=FOLD), :], HALF),
                    write, planes,
                )
                for m in range(nvel):
                    @pl.when(jnp.logical_and(me == m, slab != m))
                    def _():
                        pltpu.make_async_remote_copy(
                            src_ref=sback.at[c, slab], dst_ref=back.at[c, :, m, :],
                            send_sem=out_send.at[c, jnp.bitwise_xor(slab, m)],
                            recv_sem=out_recv.at[c, jnp.bitwise_xor(slab, m)],
                            device_id=(sp, slab), device_id_type=MESH,
                        ).start()

                    @pl.when(jnp.logical_and(me == m, slab == m))
                    def _():
                        pltpu.make_async_copy(
                            sback.at[c, m], back.at[c, :, m, :], own_out.at[c]
                        ).start()
            return carry

        lax.fori_loop(0, CHUNKS, third, 0)
        return carry

    lax.fori_loop(0, own, cell_step, 0)
    for r in range(1, nvel):
        sending(own - 1, me, r, jnp.bitwise_xor(me, r), 0).wait_send()
    for c in range(own):
        for r in range(1, nvel):
            peer = jnp.bitwise_xor(me, r)
            copy = pltpu.make_async_remote_copy(
                src_ref=sback.at[c, peer], dst_ref=back.at[c, :, 0, :],
                send_sem=out_send.at[c, r], recv_sem=out_recv.at[c, r],
                device_id=(sp, peer), device_id_type=MESH,
            )
            copy.wait_send()
            copy.wait_recv()
        pltpu.make_async_copy(sback.at[c, me], back.at[c, :, 0, :], own_out.at[c]).wait()
        cut = slice(c * nvel, (c + 1) * nvel)
        for z in range(planes):
            out[z, cut, :] = out[z, cut, :] + back[c, z]


def solution(mesh):
    nspace, nvel = mesh.shape["space"], mesh.shape["vel"]
    tables = build_tables()

    def body(distribution, collision_rate, face_flags):
        cells, planes, width = distribution.shape
        own = cells // nvel
        size = (NV * FOLD, LANES)
        spare = 8 * FOLD
        f32 = jnp.float32
        dma = pltpu.SemaphoreType.DMA
        result = pl.pallas_call(
            functools.partial(step_kernel, nspace, nvel, nspace * cells),
            out_shape=jax.ShapeDtypeStruct((planes, cells, width), f32),
            in_specs=[pl.BlockSpec(memory_space=pltpu.HBM)] * (3 + len(tables)),
            out_specs=pl.BlockSpec(memory_space=pltpu.VMEM),
            scratch_shapes=[
                pltpu.VMEM((planes, cells, width), f32),
                pltpu.VMEM((own, nvel, planes, width), f32),
                pltpu.VMEM((own, nvel, planes, width), f32),
                pltpu.VMEM((own, planes, nvel, width), f32),
                pltpu.VMEM((2, planes, width // 2), f32),
                pltpu.VMEM((NV * FOLD + spare, LANES), f32),
                pltpu.VMEM(size, f32),
                pltpu.VMEM((4,) + size, f32),
                pltpu.VMEM((2,) + size, f32),
                pltpu.VMEM((6,) + size, f32),
                pltpu.VMEM((ROWS + spare, LANES), f32),
                pltpu.SMEM((cells,), f32),
                pltpu.SMEM((nspace * cells,), jnp.int32),
                *[pltpu.VMEM(t.shape, t.dtype) for t in tables],
                dma((own + 4,)),
                dma((own, nvel)),
                dma((own, nvel)),
                dma((own, nvel)),
                dma((own, nvel)),
                dma((own,)),
                dma((own,)),
                dma((2,)),
                dma((2,)),
            ],
            compiler_params=pltpu.CompilerParams(
                collective_id=0, has_side_effects=True, vmem_limit_bytes=53 * 1024 * 1024
            ),
            cost_estimate=pl.CostEstimate(
                flops=10**9, bytes_accessed=10 * 2**20, transcendentals=0
            ),
        )(
            jnp.transpose(distribution, (1, 0, 2)), collision_rate, face_flags,
            *[jnp.asarray(t) for t in tables],
        )
        return jnp.transpose(result, (1, 0, 2))

    return jax.shard_map(
        body,
        mesh=mesh,
        in_specs=(P("space", "vel", None), P("space"), P()),
        out_specs=P("space", "vel", None),
        check_vma=False,
    )
```
